512 devices in a mesh: tok: 32 (over z_lo, y), store: 16 (over z_hi, x, core).
Axes of the slice: x: 4, y: 8, z: 8 (z_hi: 2, z_lo: 4; z = z_hi * 4 + z_lo), core: 2. Of those that a mesh axis runs over, the one named last changes fastest.
Arguments:
- activations: bfloat16 [32, 1024, 14336], P('store', 'tok'), may hold values from -6 to 6
- out_grads: bfloat16 [32, 1024, 4096], P('store', 'tok'), may hold values from -6 to 6
- validity: int32 [32, 1024], P('store', 'tok'), may hold values 0 or 1
- proj_in: bfloat16 [14336, 64], P('tok'), may hold values from -0.046875 to 0.046875
- proj_out: bfloat16 [4096, 64], P('tok'), may hold values from -0.09375 to 0.09375
- precond: bfloat16 [4096, 4096], P(('tok', 'store')), may hold values from -0.05 to 2.05, as said below
- queries: bfloat16 [1024, 4096], P('store'), may hold values from -0.09375 to 0.09375
- store_rows: float32 [65536, 4096], P(('tok', 'store')), may hold values from -6 to 6
- plan: int32 [16, 512], P(None, ('tok', 'store')), may hold values 0 or 1
Outputs:
- scores: float32 [1024, 65536], P(None, ('tok', 'store'))
- precond_docs: float32 [32, 4096], P('store', 'tok')
- doc_scores: float32 [1024, 32], P('store')
The draws below stay inside these ranges and needn't reach their ends.
Inputs may be any that keep to these rules, and one draw needn't show every extreme that they name: `precond`: symmetric positive definite. `validity`: 1 marks a real token. `plan`: 1 where the query block is scored against the store block.
All inputs are finite; a program needn't handle non-finite values. No bound on the sum of `validity` on one device may be relied on, other than what follows from the above.
Results may differ from the reference program's by a relative error of at most 0.0049.
Values may be sent and summed in bfloat16 or wider, within the bound.
A program may use at most 64 MiB of HBM per device.

```python
import math
import jax
import jax.numpy as jnp
from jax import lax

D = 4096
FF = 14336
R_IN = 64
R_OUT = 64
K = 4096
DOC_LEN = 1024
DOCS = 32
Q_DEV = 64
Q = 1024
R_DEV = 128
ROWS = 65536
N_TOK = 32
N_STORE = 16


def draw_precond(key, part):
    noise_key = jax.random.fold_in(key, 11)
    diag_key = jax.random.fold_in(key, 23)
    noise = jax.random.normal(noise_key, (K, K), jnp.float32)
    noise = (noise + noise.T) * (0.006 / math.sqrt(2.0))
    diagonal = jax.random.uniform(diag_key, (K,), jnp.float32, 1.0, 2.0)
    return (noise + jnp.diag(diagonal)).astype(jnp.bfloat16)


def plant(array, rng, least, high):
    extent = array.shape
    place = [jax.random.randint(jax.random.fold_in(rng, axis), (), 0, extent[axis]) for axis in range(len(extent))]
    array = array.at[tuple(place)].set(least)
    longest = extent.index(max(extent))
    place[longest] = (place[longest] + 1) % extent[longest]
    return array.at[tuple(place)].set(high)


def block_scale(rng, shape, split, least, top_value):
    def one(position, parts):
        draws = jax.random.uniform(jax.random.fold_in(jax.random.fold_in(rng, 6), position), (parts,), jnp.float32, least / len(split), top_value / len(split))
        return jnp.repeat(jnp.exp(draws), shape[position] // parts).reshape((-1,) + (1,) * (len(shape) - position - 1))

    factor_of = one(*split[0])
    for cut in split[1:]:
        factor_of = factor_of * one(*cut)
    return factor_of


def normal_values(own_key, dims, scale, reach, pieces=(), held_as=jnp.bfloat16):
    loudness = block_scale(own_key, dims, pieces, -0.22, 0.18) if pieces else 1.0
    values = jax.random.normal(own_key, dims, jnp.float32) * scale * loudness
    return jnp.minimum(jnp.maximum(values, -reach), reach).astype(held_as)


def setup_inputs(seed: int = 0) -> dict:
    streams_of = jax.random.split(jax.random.key(seed), 10)
    return {
        "activations": normal_values(streams_of[0], (DOCS, DOC_LEN, FF), 1.0, 6.0, ((0, 16), (1, 32))),
        "out_grads": normal_values(streams_of[1], (DOCS, DOC_LEN, D), 1.0, 6.0, ((0, 16), (1, 32))),
        "validity": plant((jax.random.randint(streams_of[2], (DOCS, DOC_LEN), 0, 4) < 3).astype(jnp.int32), jax.random.fold_in(streams_of[2], 1), 0, 1),
        "proj_in": normal_values(streams_of[3], (FF, R_IN), FF ** -0.5, 0.046875, ((0, 32),)),
        "proj_out": normal_values(streams_of[4], (D, R_OUT), D ** -0.5, 0.09375, ((0, 32),)),
        "precond": draw_precond(jax.random.fold_in(streams_of[9], 71), 0),
        "queries": normal_values(streams_of[6], (Q, K), K ** -0.5, 0.09375, ((0, 16),)),
        "store_rows": normal_values(streams_of[7], (ROWS, K), 1.0, 6.0, ((0, 512),), jnp.float32),
        "plan": plant((jax.random.randint(streams_of[8], (N_STORE, N_TOK * N_STORE), 0, 4) < 3).astype(jnp.int32), jax.random.fold_in(streams_of[8], 1), 0, 1),
    }


def reference(activations, out_grads, validity, proj_in, proj_out, precond, queries, store_rows, plan):

    def project_doc(inputs):
        doc_acts, doc_grads_in, doc_valid = inputs
        left_proj = jnp.dot(doc_acts, proj_in, preferred_element_type=jnp.float32).astype(jnp.bfloat16)
        right_proj = jnp.dot(doc_grads_in, proj_out, preferred_element_type=jnp.float32).astype(jnp.bfloat16)
        masked = right_proj.astype(jnp.float32) * doc_valid.astype(jnp.float32)[:, None]
        outer = jnp.dot(masked.T, left_proj.astype(jnp.float32), precision=lax.Precision.HIGHEST)
        return outer.reshape(-1)
    summed = lax.map(project_doc, (activations, out_grads, validity))
    norm_scale = 1.0 / math.sqrt(DOC_LEN)
    doc_grads = (summed * norm_scale).astype(jnp.bfloat16)
    precond_docs = jnp.dot(doc_grads, precond, preferred_element_type=jnp.float32)
    wide_queries = queries.astype(jnp.float32)
    doc_scores = jnp.dot(wide_queries, precond_docs.T, precision=lax.Precision.HIGHEST)
    raw_scores = jnp.dot(wide_queries, store_rows.T, precision=lax.Precision.HIGHEST)
    weights = jnp.repeat(jnp.repeat(plan, Q_DEV, axis=0), R_DEV, axis=1).astype(jnp.float32)
    scores = raw_scores * weights
    return (scores, precond_docs, doc_scores)
```

```python
import functools
import math

import jax
import jax.numpy as jnp
from jax import lax
from jax.experimental import pallas as pl
from jax.experimental.pallas import tpu as pltpu
from jax.sharding import PartitionSpec as P

MESH = pl.DeviceIdType.MESH
NT, NS = 32, 16
WIN = 512
PW = 640
QCOLS = 4096
F32 = jnp.float32
BF16 = jnp.bfloat16

UP = [(0, 0), (0, -1), (0, 1), (0, 2)] + [(-k, d) for k in (1, 2) for d in (0, -1, 1, 2)] + [(-3, 0), (-3, -1)]
DN = [(0, 0), (0, 1), (0, -1), (0, 2)] + [(k, d) for k in (1, 2) for d in (0, 1, -1, 2)] + [(3, 1), (3, 2)]
NY = len(UP)
NSPLIT = 2
NZ = 8 * NSPLIT
ZCOLS = QCOLS // NSPLIT
PLAN_Y = 0
PLAN_RS = 7
PLAN_AG = 6


def nt_dot(a, b):
    return lax.dot_general(a, b, (((1,), (1,)), ((), ())), preferred_element_type=F32)


def kernel(
    plan_ref, valid_ref, pt_ref, act_ref, og_ref, prec_ref, q_ref, rows_ref,
    scores_ref, pdoc_ref, dsc_ref,
    ptall, act, og, rows, rowsb, qall, rall, part, rsbuf, gown, gt, gs, ary, arz, arsrc, arsrc2, qp,
    lsem, pz_r, pyu_r, pyd_r, xs_r, zu_r, zd_r, one_r, snd,
):
    t = lax.axis_index("tok")
    s = lax.axis_index("store")
    zl, y = t // 8, t % 8
    zh, x, c = s // 8, (s // 2) % 4, s % 2
    z = zh * 4 + zl

    def at_z(d):
        zz = (z + 8 + d) % 8
        return ((zz % 4) * 8 + y, (zz // 4) * 8 + x * 2 + c)

    def at_y(d):
        return (zl * 8 + (y + 8 + d) % 8, s)

    def at_x(d):
        return (t, zh * 8 + ((x + 4 + d) % 4) * 2 + c)

    partner = (t, zh * 8 + x * 2 + (1 - c))
    other = (1 - zh) * 8 + x * 2 + c

    def rcopy(src, dst, ss, rs, dev):
        return pltpu.make_async_remote_copy(
            src_ref=src, dst_ref=dst, send_sem=ss, recv_sem=rs, device_id=dev, device_id_type=MESH
        )

    def drain(ref, sem):
        rcopy(ref, ref, snd.at[0], sem, partner).wait_recv()

    def sent(ref, sem):
        rcopy(ref, ref, sem, one_r.at[0], partner).wait_send()

    def qsrc(k, j):
        return q_ref.at[k, :, pl.ds(j * ZCOLS, ZCOLS)]

    R_PSH, R_QSH, R_RZ, R_RX, R_RX2, R_RSH, R_RS, R_GT, R_GS, R_ARY, R_ARZ = range(11)
    (S_PZ, S_PZH, S_PY, S_PSH, S_X, S_Z, S_QSH, S_RZ, S_RX, S_RX2, S_RSH, S_RS, S_GT, S_GS, S_ARY, S_ARZ) = range(16)

    loc = []

    def lcopy(src, dst):
        cp = pltpu.make_async_copy(src, dst, lsem.at[len(loc)])
        cp.start()
        loc.append(cp)
        return cp

    l_pt = lcopy(pt_ref, ptall.at[t])
    l_pr = lcopy(prec_ref, rall.at[s])
    for k in range(4):
        for j in range(NSPLIT):
            pltpu.make_async_copy(qsrc(k, j), qall.at[s, k, j], xs_r.at[0, k, j]).start()
    l_a = [lcopy(act_ref.at[d], act.at[pl.ds(32 * d, 32)]) for d in range(2)]
    l_o = [lcopy(og_ref.at[d], og.at[pl.ds(32 * d, 32)]) for d in range(2)]
    l_r = lcopy(rows_ref, rows)

    barrier = pltpu.get_barrier_semaphore()

    def greet(dev):
        pl.semaphore_signal(barrier, inc=1, device_id=dev, device_id_type=MESH)

    greet(at_z(1))
    greet(at_z(-1))

    @pl.loop(1, NT)
    def _(k):
        greet(((t + k) % NT, s))

    @pl.loop(1, NS)
    def _(k):
        greet((t, (s + k) % NS))

    pl.semaphore_wait(barrier, NT - 1 + NS - 1 + 2)

    half = pl.ds(2 * c, 2)

    def slot(dy, dz):
        return ((zl + 4 + dz) % 4) * 8 + (y + 8 + dy) % 8

    def psend(sl, rowsl, ss, rs, dev):
        ref = ptall.at[sl, rowsl]
        rcopy(ref, ref, ss, rs, dev).start()

    def pshare(sl):
        psend(sl, half, snd.at[S_PSH], one_r.at[R_PSH], partner)

    l_pt.wait()
    psend(t, half, snd.at[S_PZ], pz_r.at[0], at_z(1))
    psend(t, half, snd.at[S_PZ], pz_r.at[1], at_z(-1))

    def pwait(sem, n=2):
        drain(ptall.at[0, pl.ds(0, n)], sem)

    for k in range(4):
        for j in range(NSPLIT):
            dst = qall.at[s, k, j]
            rcopy(qsrc(k, j), dst, snd.at[S_X], xs_r.at[2, k, j], at_x(1)).start()
            rcopy(qsrc(k, j), dst, snd.at[S_X], xs_r.at[1, k, j], at_x(-1)).start()

    rcopy(prec_ref, rall.at[s], snd.at[S_RZ], one_r.at[R_RZ], (t, other)).start()
    for d in (1, -1, 2):
        rcopy(prec_ref, rall.at[s], snd.at[S_RX], one_r.at[R_RX], at_x(d)).start()

    def need(order, k, d):
        dy, dz = order[k]
        return 0 if dy == 0 else order.index((dy + d, dz)) + 1

    got = [0, 0]

    def yrecv_to(side, n):
        order, sems, d = ((UP, pyu_r, -1), (DN, pyd_r, 1))[side]
        while got[side] < n:
            k = got[side]
            pwait(sems.at[k])
            pshare(slot(order[k][0] + d, order[k][1]))
            got[side] += 1

    def ysend(k):
        yrecv_to(0, need(UP, k, 1))
        psend(slot(*UP[k]), half, snd.at[S_PY], pyu_r.at[k], at_y(1))
        yrecv_to(1, need(DN, k, -1))
        psend(slot(*DN[k]), half, snd.at[S_PY], pyd_r.at[k], at_y(-1))

    def xorder(i):
        return i + i // 2 - 2 * (i // 3)

    def zchunk(n, group, up):
        xi, k, j = n // (2 * NSPLIT), (n // NSPLIT) % 2, n % NSPLIT
        sl = group * 8 + ((x + xorder(xi)) % 4) * 2 + c
        return qall.at[sl, k + (0 if up else 2), j]

    def qwait(i, k, j):
        if i == 0:
            pltpu.make_async_copy(qsrc(k, j), qall.at[s, k, j], xs_r.at[0, k, j]).wait()
        else:
            drain(qall.at[0, 0, 0], xs_r.at[i, k, j])

    def qshare(ref):
        rcopy(ref, ref, snd.at[S_QSH], one_r.at[R_QSH], partner).start()

    def own_group(xi, k, j):
        return qall.at[zh * 8 + ((x + [0, 1, 3, 2][xi]) % 4) * 2 + c, k, j]

    def zstep(tau):
        if tau < NZ:
            xi, k, j = tau // (2 * NSPLIT), (tau // NSPLIT) % 2, tau % NSPLIT
            for i in {0: (0,), 1: (1, 2), 2: (), 3: (3,)}[xi]:
                for kk in (k, k + 2):
                    qwait(i, kk, j)
                    qshare(own_group(i, kk, j))
            if xi == 1:
                lref = own_group(2, k, j)
                rcopy(lref, lref, snd.at[S_X], xs_r.at[3, k, j], at_x(1)).start()
                rref = own_group(1, k + 2, j)
                rcopy(rref, rref, snd.at[S_X], xs_r.at[3, k + 2, j], at_x(-1)).start()
        if tau < NZ:

            @pl.when(zl == 3)
            def _():
                ref = zchunk(tau, zh, True)
                rcopy(ref, ref, snd.at[S_Z], zu_r.at[tau], at_z(1)).start()

            @pl.when(zl == 0)
            def _():
                ref = zchunk(tau, zh, False)
                rcopy(ref, ref, snd.at[S_Z], zd_r.at[tau], at_z(-1)).start()

        u = tau - zl

        @pl.when((u >= 0) & (u < NZ))
        def _():
            ref = zchunk(u, 1 - zh, True)
            drain(ref, zu_r.at[u])

            @pl.when(zl != 3)
            def _():
                rcopy(ref, ref, snd.at[S_Z], zu_r.at[u], at_z(1)).start()

            qshare(ref)

        v = tau - 3 + zl

        @pl.when((v >= 0) & (v < NZ))
        def _():
            ref = zchunk(v, 1 - zh, False)
            drain(ref, zd_r.at[v])

            @pl.when(zl != 0)
            def _():
                rcopy(ref, ref, snd.at[S_Z], zd_r.at[v], at_z(-1)).start()

            qshare(ref)

    nsteps = NZ + 3
    zs = iter(range(nsteps))

    def zrun(n):
        for _ in range(n):
            tau = next(zs, None)
            if tau is None:
                return
            zstep(tau)

    ysend(0)
    pwait(pz_r.at[0])
    psend(slot(0, -1), pl.ds(2 * c, 1), snd.at[S_PZH], pz_r.at[2], at_z(1))
    pwait(pz_r.at[1])
    psend(slot(0, 1), pl.ds(2 * c + 1, 1), snd.at[S_PZH], pz_r.at[3], at_z(-1))
    ysend(1)
    ysend(2)
    pshare(slot(0, -1))
    pshare(slot(0, 1))
    pwait(pz_r.at[2], 1)
    pwait(pz_r.at[3], 1)
    ysend(3)
    pshare(slot(0, 2))
    for k in range(4, NY):
        ysend(k)
        if k % 4 == 0:
            zrun(PLAN_Y)
    drain(rall.at[0], one_r.at[R_RZ])
    for d in (1, -1, 2):
        rcopy(rall.at[other], rall.at[other], snd.at[S_RX2], one_r.at[R_RX2], at_x(d)).start()
    yrecv_to(0, NY)
    yrecv_to(1, NY)
    drain(rall.at[pl.ds(0, 3)], one_r.at[R_RX])

    l_r.wait()
    rowsb[...] = rows[...].astype(BF16)
    for cp in l_a + l_o:
        cp.wait()
    drain(ptall.at[pl.ds(0, NT - 1), pl.ds(0, 2)], one_r.at[R_PSH])

    def project(i, acc):
        left, right = acc
        start = pl.multiple_of(448 * i - 64 * (i % 2), 128)
        w = ptall[i].reshape(64, PW)
        left = left + nt_dot(act[:, pl.ds(start, WIN)], w[:, :WIN])
        right = right + nt_dot(w[:, WIN:], og[:, pl.ds(pl.multiple_of(128 * i, 128), 128)])
        return left, right

    zero = jnp.zeros((64, 64), F32)
    left, right = lax.fori_loop(0, NT, project, (zero, zero))
    left = left.astype(BF16)
    right = right.astype(BF16)
    r0 = lax.broadcasted_iota(jnp.int32, (64, 64), 0)
    r1 = lax.broadcasted_iota(jnp.int32, (64, 64), 1)
    pick = (r1 == 2 * (r0 % 32) + r0 // 32).astype(F32).astype(BF16)
    right = jnp.dot(pick, right, preferred_element_type=F32)
    for d in range(2):
        masked = (right * valid_ref[pl.ds(d, 1), :]).astype(BF16)
        outer = jnp.dot(masked, left, preferred_element_type=F32)
        part[:, d, :] = jnp.concatenate([outer[:32], outer[32:]], axis=1)

    @pl.loop(1, NT)
    def _(k):
        to = (t + k) % NT
        rcopy(part.at[to], rsbuf.at[t], snd.at[S_RS], one_r.at[R_RS], (to, s)).start()

    rsbuf[t] = part[t]
    zrun(PLAN_RS)
    drain(rsbuf.at[pl.ds(0, NT - 1)], one_r.at[R_RS])
    total = jnp.sum(rsbuf[...], axis=0) * (1.0 / 32.0)
    gown[...] = total.astype(BF16).astype(F32)
    gt[t] = gown[...]
    gs[s] = gown[...]

    @pl.loop(1, NS)
    def _(k):
        rcopy(gown, gs.at[s], snd.at[S_GS], one_r.at[R_GS], (t, (s + k) % NS)).start()

    @pl.loop(1, NT)
    def _(k):
        rcopy(gown, gt.at[t], snd.at[S_GT], one_r.at[R_GT], ((t + k) % NT, s)).start()

    l_pr.wait()
    drain(rall.at[pl.ds(0, 3)], one_r.at[R_RX2])

    @pl.loop(0, 8)
    def _(k):
        ref = rall.at[2 * k + c]
        rcopy(ref, ref, snd.at[S_RSH], one_r.at[R_RSH], partner).start()

    zrun(PLAN_AG)
    drain(rall.at[pl.ds(0, 8)], one_r.at[R_RSH])
    prows = rall[...].astype(F32).reshape(128, 4096).astype(BF16)
    for k in range(4):
        own_q = jnp.concatenate([qall[s, k, j] for j in range(NSPLIT)], axis=1)
        qp[pl.ds(16 * k, 16), :] = nt_dot(own_q, prows).astype(BF16)

    drain(gs.at[pl.ds(0, NS - 1)], one_r.at[R_GS])
    docs = jnp.concatenate([gs[:, 0, :], gs[:, 1, :]], axis=0)
    acc = jnp.zeros((16, 128), F32)
    d0 = lax.broadcasted_iota(jnp.int32, (128, 32), 0)
    d1 = lax.broadcasted_iota(jnp.int32, (128, 32), 1)
    for j in range(4):
        put = (d0 == 32 * j + 2 * (d1 % 16) + d1 // 16).astype(F32).astype(BF16)
        spread = jnp.dot(put, docs.astype(BF16), preferred_element_type=F32).astype(BF16)
        acc = acc + nt_dot(qp[pl.ds(16 * j, 16), :], spread)
    arsrc[...] = acc
    ary[y] = acc

    @pl.loop(1, 8)
    def _(k):
        rcopy(arsrc, ary.at[y], snd.at[S_ARY], one_r.at[R_ARY], at_y(k)).start()

    drain(gt.at[pl.ds(0, NT - 1)], one_r.at[R_GT])
    pdoc_ref[...] = nt_dot(jnp.concatenate([gt[i] for i in range(NT)], axis=1).astype(BF16), prows)

    drain(ary.at[pl.ds(0, 7)], one_r.at[R_ARY])
    acc = jnp.sum(ary[...], axis=0)
    arsrc2[...] = acc
    arz[zl] = acc

    @pl.loop(1, 4)
    def _(k):
        rcopy(arsrc2, arz.at[zl], snd.at[S_ARZ], one_r.at[R_ARZ], (((zl + k) % 4) * 8 + y, s)).start()

    zrun(nsteps)
    drain(qall.at[pl.ds(0, 8)], one_r.at[R_QSH])

    @pl.loop(0, NS // 2)
    def _(k):
        raw = jnp.zeros((128, 128), F32)
        for j in range(NSPLIT):
            blk = jnp.concatenate([qall[2 * k + h, i, j] for h in range(2) for i in range(4)], axis=0)
            raw = raw + nt_dot(blk, rowsb[:, ZCOLS * j : ZCOLS * (j + 1)])
        for h in range(2):
            w = plan_ref[2 * k + h].astype(F32)
            scores_ref[pl.ds(pl.multiple_of(128 * k + 64 * h, 64), 64), :] = raw[64 * h : 64 * h + 64] * w

    drain(arz.at[pl.ds(0, 3)], one_r.at[R_ARZ])
    acc = jnp.sum(arz[...], axis=0)
    for j in range(4):
        dsc_ref[pl.ds(16 * j, 16), :] = acc[:, 32 * j : 32 * j + 32]

    sent(ptall.at[pl.ds(0, 2), pl.ds(0, 2)], snd.at[S_PZ])
    sent(ptall.at[0, pl.ds(0, 2)], snd.at[S_PZH])
    sent(ptall.at[pl.ds(0, 2 * NY), pl.ds(0, 2)], snd.at[S_PY])
    sent(ptall.at[pl.ds(0, NT - 1), pl.ds(0, 2)], snd.at[S_PSH])
    sent(qall.at[pl.ds(0, 3)], snd.at[S_X])
    sent(qall.at[pl.ds(0, 4)], snd.at[S_Z])
    sent(qall.at[pl.ds(0, 8)], snd.at[S_QSH])
    sent(rall.at[0], snd.at[S_RZ])
    sent(rall.at[pl.ds(0, 3)], snd.at[S_RX])
    sent(rall.at[pl.ds(0, 3)], snd.at[S_RX2])
    sent(rall.at[pl.ds(0, 8)], snd.at[S_RSH])
    sent(rsbuf.at[pl.ds(0, NT - 1)], snd.at[S_RS])
    sent(gt.at[pl.ds(0, NT - 1)], snd.at[S_GT])
    sent(gs.at[pl.ds(0, NS - 1)], snd.at[S_GS])
    sent(ary.at[pl.ds(0, 7)], snd.at[S_ARY])
    sent(arz.at[pl.ds(0, 3)], snd.at[S_ARZ])


def local(activations, out_grads, validity, proj_in, proj_out, precond, queries, store_rows, plan):
    t = lax.axis_index("tok")
    pin = proj_in.T
    win = jnp.where(t % 2 == 0, jnp.pad(pin, ((0, 0), (0, 64))), jnp.pad(pin, ((0, 0), (64, 0))))
    pt = jnp.concatenate([win, proj_out.T], axis=1).reshape(4, 16, PW)
    own = jnp.eye(2, dtype=F32)[:, :, None] * validity.astype(F32)[None]
    valid = own.reshape(2, 64)
    hbm = pl.BlockSpec(memory_space=pl.ANY)
    vm = pl.BlockSpec(memory_space=pltpu.VMEM)
    sm = pl.BlockSpec(memory_space=pltpu.SMEM)
    dma = pltpu.SemaphoreType.DMA
    return pl.pallas_call(
        kernel,
        out_shape=(
            jax.ShapeDtypeStruct((1024, 128), F32),
            jax.ShapeDtypeStruct((2, 128), F32),
            jax.ShapeDtypeStruct((64, 32), F32),
        ),
        in_specs=[sm, vm, hbm, hbm, hbm, hbm, hbm, hbm],
        out_specs=(vm, vm, vm),
        scratch_shapes=[
            pltpu.VMEM((NT, 4, 16, PW), BF16),
            pltpu.VMEM((64, 14336), BF16),
            pltpu.VMEM((64, 4096), BF16),
            pltpu.VMEM((128, 4096), F32),
            pltpu.VMEM((128, 4096), BF16),
            pltpu.VMEM((NS, 4, NSPLIT, 16, ZCOLS), BF16),
            pltpu.VMEM((NS, 8, 4096), BF16),
            pltpu.VMEM((NT, 2, 128), F32),
            pltpu.VMEM((NT, 2, 128), F32),
            pltpu.VMEM((2, 128), F32),
            pltpu.VMEM((NT, 2, 128), F32),
            pltpu.VMEM((NS, 2, 128), F32),
            pltpu.VMEM((8, 16, 128), F32),
            pltpu.VMEM((4, 16, 128), F32),
            pltpu.VMEM((16, 128), F32),
            pltpu.VMEM((16, 128), F32),
            pltpu.VMEM((64, 128), BF16),
            dma((7,)),
            dma((4,)),
            dma((NY,)),
            dma((NY,)),
            dma((4, 4, NSPLIT)),
            dma((NZ,)),
            dma((NZ,)),
            dma((11,)),
            dma((16,)),
        ],
        compiler_params=pltpu.CompilerParams(collective_id=0, has_side_effects=True),
        name="logra",
    )(
        plan.reshape(16),
        valid,
        pt,
        activations,
        out_grads,
        precond,
        queries.reshape(4, 16, 4096),
        store_rows,
    )


def solution(mesh):
    return jax.shard_map(
        local,
        mesh=mesh,
        in_specs=(
            P("store", "tok", None),
            P("store", "tok", None),
            P("store", "tok"),
            P("tok", None),
            P("tok", None),
            P(("tok", "store"), None),
            P("store", None),
            P(("tok", "store"), None),
            P(None, ("tok", "store")),
        ),
        out_specs=(P(None, ("tok", "store")), P("store", "tok"), P("store", None)),
        check_vma=False,
    )
```

```python
import functools
import math

import jax
import jax.numpy as jnp
from jax import lax
from jax.experimental import pallas as pl
from jax.experimental.pallas import tpu as pltpu
from jax.sharding import PartitionSpec as P

MESH = pl.DeviceIdType.MESH
NT, NS = 32, 16
WIN = 512
PW = 640
QCOLS = 4096
F32 = jnp.float32
BF16 = jnp.bfloat16

UP = [(0, 0), (0, -1), (0, 1), (0, 2)] + [(-k, d) for k in (1, 2) for d in (0, -1, 1, 2)] + [(-3, 0), (-3, -1)]
DN = [(0, 0), (0, 1), (0, -1), (0, 2)] + [(k, d) for k in (1, 2) for d in (0, 1, -1, 2)] + [(3, 1), (3, 2)]
NY = len(UP)
NSPLIT = 2
NZ = 8 * NSPLIT
ZCOLS = QCOLS // NSPLIT
LAG = 2
PLAN_Y = 1
PLAN_RS = 6
PLAN_AG = 4


def nt_dot(a, b):
    return lax.dot_general(a, b, (((1,), (1,)), ((), ())), preferred_element_type=F32)


def kernel(
    plan_ref, valid_ref, pin_ref, pout_ref, act_ref, og_ref, prec_ref, q_ref, rows_ref,
    scores_ref, pdoc_ref, dsc_ref,
    ptall, act, og, rows, rowsb, qall, rall, part, rsbuf, gown, gt, gs, ary, arz, arsrc, arsrc2, qp,
    lsem, pz_r, pyu_r, pyd_r, xs_r, zu_r, zd_r, one_r, snd,
):
    t = lax.axis_index("tok")
    s = lax.axis_index("store")
    zl, y = t // 8, t % 8
    zh, x, c = s // 8, (s // 2) % 4, s % 2
    z = zh * 4 + zl

    def at_z(d):
        zz = (z + 8 + d) % 8
        return ((zz % 4) * 8 + y, (zz // 4) * 8 + x * 2 + c)

    def at_y(d):
        return (zl * 8 + (y + 8 + d) % 8, s)

    def at_x(d):
        return (t, zh * 8 + ((x + 4 + d) % 4) * 2 + c)

    partner = (t, zh * 8 + x * 2 + (1 - c))
    other = (1 - zh) * 8 + x * 2 + c

    def rcopy(src, dst, ss, rs, dev):
        return pltpu.make_async_remote_copy(
            src_ref=src, dst_ref=dst, send_sem=ss, recv_sem=rs, device_id=dev, device_id_type=MESH
        )

    def drain(ref, sem):
        rcopy(ref, ref, snd.at[0], sem, partner).wait_recv()

    def sent(ref, sem):
        rcopy(ref, ref, sem, one_r.at[0], partner).wait_send()

    def qsrc(k, j):
        return q_ref.at[k, :, pl.ds(j * ZCOLS, ZCOLS)]

    R_PSH, R_PSH2, R_QSA, R_QSB, R_RZ, R_RX, R_RX2, R_RSH, R_RS, R_GT, R_GS, R_ARY, R_ARZ = range(13)
    (S_PZ, S_PZH, S_PY, S_PSH, S_X, S_Z, S_QSH, S_RZ, S_RX, S_RX2, S_RSH, S_RS, S_GT, S_GS, S_ARY, S_ARZ) = range(16)

    loc = []

    def lcopy(src, dst):
        cp = pltpu.make_async_copy(src, dst, lsem.at[len(loc)])
        cp.start()
        loc.append(cp)
        return cp

    l_pr = lcopy(prec_ref, rall.at[s])
    for k in range(4):
        for j in range(NSPLIT):
            pltpu.make_async_copy(qsrc(k, j), qall.at[s, k, j], xs_r.at[0, k, j]).start()
    l_a = [lcopy(act_ref.at[d], act.at[pl.ds(32 * d, 32)]) for d in range(2)]
    l_o = [lcopy(og_ref.at[d], og.at[pl.ds(32 * d, 32)]) for d in range(2)]
    l_r = lcopy(rows_ref, rows)

    barrier = pltpu.get_barrier_semaphore()

    def greet(dev):
        pl.semaphore_signal(barrier, inc=1, device_id=dev, device_id_type=MESH)

    greet(at_z(1))
    greet(at_z(-1))

    @pl.loop(1, NT)
    def _(k):
        greet(((t + k) % NT, s))

    @pl.loop(1, NS)
    def _(k):
        greet((t, (s + k) % NS))

    win = pin_ref[...]
    gap = jnp.zeros((64, WIN - 448), BF16)

    @pl.when(t % 2 == 0)
    def _():
        ptall[t, :, :, :WIN] = jnp.concatenate([win, gap], axis=1).reshape(4, 16, WIN)

    @pl.when(t % 2 == 1)
    def _():
        ptall[t, :, :, :WIN] = jnp.concatenate([gap, win], axis=1).reshape(4, 16, WIN)

    ptall[t, :, :, WIN:] = pout_ref[...].reshape(4, 16, PW - WIN)
    pl.semaphore_wait(barrier, NT - 1 + NS - 1 + 2)

    half = pl.ds(2 * c, 2)

    def slot(dy, dz):
        return ((zl + 4 + dz) % 4) * 8 + (y + 8 + dy) % 8

    def psend(sl, rowsl, ss, rs, dev):
        ref = ptall.at[sl, rowsl]
        rcopy(ref, ref, ss, rs, dev).start()

    def pshare(sl, group=None):
        psend(sl, half, snd.at[S_PSH], one_r.at[R_PSH if group is None else group], partner)

    psend(t, half, snd.at[S_PZ], pz_r.at[0], at_z(1))
    psend(t, half, snd.at[S_PZ], pz_r.at[1], at_z(-1))

    def pwait(sem, n=2):
        drain(ptall.at[0, pl.ds(0, n)], sem)

    for k in (0, 2, 1, 3):
        for j in range(NSPLIT):
            dst = qall.at[s, k, j]
            rcopy(qsrc(k, j), dst, snd.at[S_X], xs_r.at[2, k, j], at_x(1)).start()
            rcopy(qsrc(k, j), dst, snd.at[S_X], xs_r.at[1, k, j], at_x(-1)).start()

    rcopy(prec_ref, rall.at[s], snd.at[S_RZ], one_r.at[R_RZ], (t, other)).start()
    for d in (1, -1, 2):
        rcopy(prec_ref, rall.at[s], snd.at[S_RX], one_r.at[R_RX], at_x(d)).start()

    def need(order, k, d):
        dy, dz = order[k]
        return 0 if dy == 0 else order.index((dy + d, dz)) + 1

    got = [0, 0]

    def yrecv_to(side, n):
        order, sems, d = ((UP, pyu_r, -1), (DN, pyd_r, 1))[side]
        while got[side] < n:
            k = got[side]
            pwait(sems.at[k])
            pshare(slot(order[k][0] + d, order[k][1]), R_PSH if k < 8 else R_PSH2)
            got[side] += 1

    def ysend(k):
        yrecv_to(0, need(UP, k, 1))
        psend(slot(*UP[k]), half, snd.at[S_PY], pyu_r.at[k], at_y(1))
        yrecv_to(1, need(DN, k, -1))
        psend(slot(*DN[k]), half, snd.at[S_PY], pyd_r.at[k], at_y(-1))

    def xorder(i):
        return i + i // 2 - 2 * (i // 3)

    def zchunk(n, group, up):
        xi, k, j = n // (2 * NSPLIT), (n // NSPLIT) % 2, n % NSPLIT
        sl = group * 8 + ((x + xorder(xi)) % 4) * 2 + c
        return qall.at[sl, k + (0 if up else 2), j]

    def qwait(i, k, j):
        if i == 0:
            pltpu.make_async_copy(qsrc(k, j), qall.at[s, k, j], xs_r.at[0, k, j]).wait()
        else:
            drain(qall.at[0, 0, 0], xs_r.at[i, k, j])

    def qshare(ref, group):
        rcopy(ref, ref, snd.at[S_QSH], one_r.at[group], partner).start()

    def own_group(xi, k, j):
        return qall.at[zh * 8 + ((x + [0, 1, 3, 2][xi]) % 4) * 2 + c, k, j]

    def zstep(tau):
        if tau < NZ:
            xi, k, j = tau // (2 * NSPLIT), (tau // NSPLIT) % 2, tau % NSPLIT
            for i in {0: (0,), 1: (1, 2), 2: (), 3: (3,)}[xi]:
                for kk in (k, k + 2):
                    qwait(i, kk, j)
                    qshare(own_group(i, kk, j), R_QSA)
            if xi == 1:
                lref = own_group(2, k, j)
                rcopy(lref, lref, snd.at[S_X], xs_r.at[3, k, j], at_x(1)).start()
                rref = own_group(1, k + 2, j)
                rcopy(rref, rref, snd.at[S_X], xs_r.at[3, k + 2, j], at_x(-1)).start()
        if tau < NZ:

            @pl.when(zl == 3)
            def _():
                ref = zchunk(tau, zh, True)
                rcopy(ref, ref, snd.at[S_Z], zu_r.at[tau], at_z(1)).start()

            @pl.when(zl == 0)
            def _():
                ref = zchunk(tau, zh, False)
                rcopy(ref, ref, snd.at[S_Z], zd_r.at[tau], at_z(-1)).start()

        u = tau - LAG * (zl + 1)

        @pl.when((u >= 0) & (u < NZ))
        def _():
            ref = zchunk(u, 1 - zh, True)
            drain(ref, zu_r.at[u])

            @pl.when(zl != 3)
            def _():
                rcopy(ref, ref, snd.at[S_Z], zu_r.at[u], at_z(1)).start()

            qshare(ref, R_QSB)

        v = tau - LAG * (4 - zl)

        @pl.when((v >= 0) & (v < NZ))
        def _():
            ref = zchunk(v, 1 - zh, False)
            drain(ref, zd_r.at[v])

            @pl.when(zl != 0)
            def _():
                rcopy(ref, ref, snd.at[S_Z], zd_r.at[v], at_z(-1)).start()

            qshare(ref, R_QSB)

    nsteps = NZ + 4 * LAG
    zs = iter(range(nsteps))

    def zrun(n):
        for _ in range(n):
            tau = next(zs, None)
            if tau is None:
                return
            zstep(tau)

    def score(group):
        @pl.loop(0, 4)
        def _(k):
            sl = group * 8 + 2 * k
            raw = jnp.zeros((128, 128), F32)
            for j in range(NSPLIT):
                blk = jnp.concatenate([qall[sl + h, i, j] for h in range(2) for i in range(4)], axis=0)
                raw = raw + nt_dot(blk, rowsb[:, ZCOLS * j : ZCOLS * (j + 1)])
            for h in range(2):
                w = plan_ref[sl + h].astype(F32)
                scores_ref[pl.ds(pl.multiple_of(64 * (sl + h), 64), 64), :] = raw[64 * h : 64 * h + 64] * w

    ysend(0)
    pwait(pz_r.at[0])
    psend(slot(0, -1), pl.ds(2 * c, 1), snd.at[S_PZH], pz_r.at[2], at_z(1))
    pwait(pz_r.at[1])
    psend(slot(0, 1), pl.ds(2 * c + 1, 1), snd.at[S_PZH], pz_r.at[3], at_z(-1))
    ysend(1)
    ysend(2)
    pshare(slot(0, -1))
    pshare(slot(0, 1))
    pwait(pz_r.at[2], 1)
    pwait(pz_r.at[3], 1)
    ysend(3)
    pshare(slot(0, 2))
    for k in range(4, NY):
        ysend(k)
        zrun(PLAN_Y)
    drain(rall.at[0], one_r.at[R_RZ])
    for d in (1, -1, 2):
        rcopy(rall.at[other], rall.at[other], snd.at[S_RX2], one_r.at[R_RX2], at_x(d)).start()
    l_r.wait()
    rowsb[...] = rows[...].astype(BF16)
    for cp in l_a + l_o:
        cp.wait()

    def project(acc, dys):
        left, right = acc
        for dy in dys:
            for dz in (0, 1, 2, 3):
                i = slot(dy, dz)
                start = pl.multiple_of(448 * i - 64 * (i % 2), 128)
                w = ptall[i].reshape(64, PW)
                left = left + nt_dot(act[:, pl.ds(start, WIN)], w[:, :WIN])
                right = right + nt_dot(w[:, WIN:], og[:, pl.ds(pl.multiple_of(128 * i, 128), 128)])
        return left, right

    drain(ptall.at[pl.ds(0, 19), pl.ds(0, 2)], one_r.at[R_PSH])
    acc = project((jnp.zeros((64, 64), F32), jnp.zeros((64, 64), F32)), (0, -1, 1, -2, 2))
    yrecv_to(0, NY)
    yrecv_to(1, NY)
    drain(rall.at[pl.ds(0, 3)], one_r.at[R_RX])
    drain(ptall.at[pl.ds(0, 12), pl.ds(0, 2)], one_r.at[R_PSH2])
    left, right = project(acc, (-3, 3, 4))
    left = left.astype(BF16)
    right = right.astype(BF16)
    r0 = lax.broadcasted_iota(jnp.int32, (64, 64), 0)
    r1 = lax.broadcasted_iota(jnp.int32, (64, 64), 1)
    pick = (r1 == 2 * (r0 % 32) + r0 // 32).astype(F32).astype(BF16)
    right = jnp.dot(pick, right, preferred_element_type=F32)
    for d in range(2):
        live = valid_ref[pl.ds(d, 1), :].astype(F32)
        rest = jnp.zeros((1, 32), F32)
        masked = (right * jnp.concatenate([live, rest] if d == 0 else [rest, live], axis=1)).astype(BF16)
        outer = jnp.dot(masked, left, preferred_element_type=F32)
        part[:, d, :] = jnp.concatenate([outer[:32], outer[32:]], axis=1)

    @pl.loop(1, NT)
    def _(k):
        to = (t + k) % NT
        rcopy(part.at[to], rsbuf.at[t], snd.at[S_RS], one_r.at[R_RS], (to, s)).start()

    rsbuf[t] = part[t]
    zrun(PLAN_RS)
    drain(qall.at[pl.ds(0, 4)], one_r.at[R_QSA])
    score(zh)
    drain(rsbuf.at[pl.ds(0, NT - 1)], one_r.at[R_RS])
    total = jnp.sum(rsbuf[...], axis=0) * (1.0 / 32.0)
    gown[...] = total.astype(BF16).astype(F32)
    gt[t] = gown[...]
    gs[s] = gown[...]

    @pl.loop(1, NS)
    def _(k):
        rcopy(gown, gs.at[s], snd.at[S_GS], one_r.at[R_GS], (t, (s + k) % NS)).start()

    @pl.loop(1, NT)
    def _(k):
        rcopy(gown, gt.at[t], snd.at[S_GT], one_r.at[R_GT], ((t + k) % NT, s)).start()

    l_pr.wait()
    drain(rall.at[pl.ds(0, 3)], one_r.at[R_RX2])

    @pl.loop(0, 8)
    def _(k):
        ref = rall.at[2 * k + c]
        rcopy(ref, ref, snd.at[S_RSH], one_r.at[R_RSH], partner).start()

    zrun(PLAN_AG)
    drain(rall.at[pl.ds(0, 8)], one_r.at[R_RSH])
    prows = rall[...].astype(F32).reshape(128, 4096).astype(BF16)
    for k in range(4):
        own_q = jnp.concatenate([qall[s, k, j] for j in range(NSPLIT)], axis=1)
        qp[pl.ds(16 * k, 16), :] = nt_dot(own_q, prows).astype(BF16)

    drain(gs.at[pl.ds(0, NS - 1)], one_r.at[R_GS])
    docs = jnp.concatenate([gs[:, 0, :], gs[:, 1, :]], axis=0)
    acc = jnp.zeros((16, 128), F32)
    d0 = lax.broadcasted_iota(jnp.int32, (128, 32), 0)
    d1 = lax.broadcasted_iota(jnp.int32, (128, 32), 1)
    for j in range(4):
        put = (d0 == 32 * j + 2 * (d1 % 16) + d1 // 16).astype(F32).astype(BF16)
        spread = jnp.dot(put, docs.astype(BF16), preferred_element_type=F32).astype(BF16)
        acc = acc + nt_dot(qp[pl.ds(16 * j, 16), :], spread)
    arsrc[...] = acc
    ary[y] = acc

    @pl.loop(1, 8)
    def _(k):
        rcopy(arsrc, ary.at[y], snd.at[S_ARY], one_r.at[R_ARY], at_y(k)).start()

    drain(gt.at[pl.ds(0, NT - 1)], one_r.at[R_GT])
    pdoc_ref[...] = nt_dot(jnp.concatenate([gt[i] for i in range(NT)], axis=1).astype(BF16), prows)

    drain(ary.at[pl.ds(0, 7)], one_r.at[R_ARY])
    acc = jnp.sum(ary[...], axis=0)
    arsrc2[...] = acc
    arz[zl] = acc

    @pl.loop(1, 4)
    def _(k):
        rcopy(arsrc2, arz.at[zl], snd.at[S_ARZ], one_r.at[R_ARZ], (((zl + k) % 4) * 8 + y, s)).start()

    zrun(nsteps)
    drain(qall.at[pl.ds(0, 4)], one_r.at[R_QSB])
    score(1 - zh)

    drain(arz.at[pl.ds(0, 3)], one_r.at[R_ARZ])
    acc = jnp.sum(arz[...], axis=0)
    for j in range(4):
        dsc_ref[pl.ds(16 * j, 16), :] = acc[:, 32 * j : 32 * j + 32]

    sent(ptall.at[pl.ds(0, 2), pl.ds(0, 2)], snd.at[S_PZ])
    sent(ptall.at[0, pl.ds(0, 2)], snd.at[S_PZH])
    sent(ptall.at[pl.ds(0, 2 * NY), pl.ds(0, 2)], snd.at[S_PY])
    sent(ptall.at[pl.ds(0, NT - 1), pl.ds(0, 2)], snd.at[S_PSH])
    sent(qall.at[pl.ds(0, 3)], snd.at[S_X])
    sent(qall.at[pl.ds(0, 4)], snd.at[S_Z])
    sent(qall.at[pl.ds(0, 8)], snd.at[S_QSH])
    sent(rall.at[0], snd.at[S_RZ])
    sent(rall.at[pl.ds(0, 3)], snd.at[S_RX])
    sent(rall.at[pl.ds(0, 3)], snd.at[S_RX2])
    sent(rall.at[pl.ds(0, 8)], snd.at[S_RSH])
    sent(rsbuf.at[pl.ds(0, NT - 1)], snd.at[S_RS])
    sent(gt.at[pl.ds(0, NT - 1)], snd.at[S_GT])
    sent(gs.at[pl.ds(0, NS - 1)], snd.at[S_GS])
    sent(ary.at[pl.ds(0, 7)], snd.at[S_ARY])
    sent(arz.at[pl.ds(0, 3)], snd.at[S_ARZ])


def local(activations, out_grads, validity, proj_in, proj_out, precond, queries, store_rows, plan):
    hbm = pl.BlockSpec(memory_space=pl.ANY)
    vm = pl.BlockSpec(memory_space=pltpu.VMEM)
    sm = pl.BlockSpec(memory_space=pltpu.SMEM)
    dma = pltpu.SemaphoreType.DMA
    return pl.pallas_call(
        kernel,
        out_shape=(
            jax.ShapeDtypeStruct((1024, 128), F32),
            jax.ShapeDtypeStruct((2, 128), F32),
            jax.ShapeDtypeStruct((64, 32), F32),
        ),
        in_specs=[sm, vm, vm, vm, hbm, hbm, hbm, hbm, hbm],
        out_specs=(vm, vm, vm),
        scratch_shapes=[
            pltpu.VMEM((NT, 4, 16, PW), BF16),
            pltpu.VMEM((64, 14336), BF16),
            pltpu.VMEM((64, 4096), BF16),
            pltpu.VMEM((128, 4096), F32),
            pltpu.VMEM((128, 4096), BF16),
            pltpu.VMEM((NS, 4, NSPLIT, 16, ZCOLS), BF16),
            pltpu.VMEM((NS, 8, 4096), BF16),
            pltpu.VMEM((NT, 2, 128), F32),
            pltpu.VMEM((NT, 2, 128), F32),
            pltpu.VMEM((2, 128), F32),
            pltpu.VMEM((NT, 2, 128), F32),
            pltpu.VMEM((NS, 2, 128), F32),
            pltpu.VMEM((8, 16, 128), F32),
            pltpu.VMEM((4, 16, 128), F32),
            pltpu.VMEM((16, 128), F32),
            pltpu.VMEM((16, 128), F32),
            pltpu.VMEM((64, 128), BF16),
            dma((6,)),
            dma((4,)),
            dma((NY,)),
            dma((NY,)),
            dma((4, 4, NSPLIT)),
            dma((NZ,)),
            dma((NZ,)),
            dma((13,)),
            dma((16,)),
        ],
        compiler_params=pltpu.CompilerParams(collective_id=0, has_side_effects=True),
        name="logra",
    )(
        plan.reshape(16),
        validity,
        proj_in.T,
        proj_out.T,
        activations,
        out_grads,
        precond,
        queries.reshape(4, 16, 4096),
        store_rows,
    )


def solution(mesh):
    return jax.shard_map(
        local,
        mesh=mesh,
        in_specs=(
            P("store", "tok", None),
            P("store", "tok", None),
            P("store", "tok"),
            P("tok", None),
            P("tok", None),
            P(("tok", "store"), None),
            P("store", None),
            P(("tok", "store"), None),
            P(None, ("tok", "store")),
        ),
        out_specs=(P(None, ("tok", "store")), P("store", "tok"), P("store", None)),
        check_vma=False,
    )
```

```python
import functools
import math

import jax
import jax.numpy as jnp
from jax import lax
from jax.experimental import pallas as pl
from jax.experimental.pallas import tpu as pltpu
from jax.sharding import PartitionSpec as P

MESH = pl.DeviceIdType.MESH
NT, NS = 32, 16
WIN = 512
PW = 640
QCOLS = 4096
F32 = jnp.float32
BF16 = jnp.bfloat16

UP = [(0, 0), (0, -1), (0, 1), (0, 2)] + [(-k, d) for k in (1, 2) for d in (0, -1, 1, 2)] + [(-3, 0), (-3, -1)]
DN = [(0, 0), (0, 1), (0, -1), (0, 2)] + [(k, d) for k in (1, 2) for d in (0, 1, -1, 2)] + [(3, 1), (3, 2)]
NY = len(UP)
NSPLIT = 2
NZ = 8 * NSPLIT
ZCOLS = QCOLS // NSPLIT
LAG = 3
PLAN_Y = 1
PLAN_RS = 3
PLAN_AG = 4
PLAN_AR = 3


def nt_dot(a, b):
    return lax.dot_general(a, b, (((1,), (1,)), ((), ())), preferred_element_type=F32)


def kernel(
    plan_ref, valid_ref, pin_ref, pout_ref, act_ref, og_ref, prec_ref, q_ref, rows_ref,
    scores_ref, pdoc_ref, dsc_ref,
    ptall, act, og, rows, rowsb, qall, rall, part, rsbuf, gown, gt, gs, ary, arz, arsrc, arsrc2,
    lsem, pz_r, pyu_r, pyd_r, xs_r, zu_r, zd_r, one_r, snd,
):
    t = lax.axis_index("tok")
    s = lax.axis_index("store")
    zl, y = t // 8, t % 8
    zh, x, c = s // 8, (s // 2) % 4, s % 2
    z = zh * 4 + zl

    def at_z(d):
        zz = (z + 8 + d) % 8
        return ((zz % 4) * 8 + y, (zz // 4) * 8 + x * 2 + c)

    def at_y(d):
        return (zl * 8 + (y + 8 + d) % 8, s)

    def at_x(d):
        return (t, zh * 8 + ((x + 4 + d) % 4) * 2 + c)

    partner = (t, zh * 8 + x * 2 + (1 - c))
    other = (1 - zh) * 8 + x * 2 + c

    def rcopy(src, dst, ss, rs, dev):
        return pltpu.make_async_remote_copy(
            src_ref=src, dst_ref=dst, send_sem=ss, recv_sem=rs, device_id=dev, device_id_type=MESH
        )

    def drain(ref, sem):
        rcopy(ref, ref, snd.at[0], sem, partner).wait_recv()

    def sent(ref, sem):
        rcopy(ref, ref, sem, one_r.at[0], partner).wait_send()

    def qsrc(k, j):
        return q_ref.at[k, :, pl.ds(j * ZCOLS, ZCOLS)]

    R_PSH, R_PSH2, R_QSA, R_QSB, R_RZ, R_RX, R_RX2, R_RSH, R_RS, R_GT, R_GS, R_ARY, R_ARZ = range(13)
    (S_PZ, S_PZH, S_PY, S_PSH, S_X, S_Z, S_QSH, S_RZ, S_RX, S_RX2, S_RSH, S_RS, S_GT, S_GS, S_ARY, S_ARZ) = range(16)

    loc = []

    def lcopy(src, dst):
        cp = pltpu.make_async_copy(src, dst, lsem.at[len(loc)])
        cp.start()
        loc.append(cp)
        return cp

    l_pr = lcopy(prec_ref, rall.at[s])
    for k in range(4):
        for j in range(NSPLIT):
            pltpu.make_async_copy(qsrc(k, j), qall.at[s, k, j], xs_r.at[0, k, j]).start()
    l_a = [lcopy(act_ref.at[d], act.at[pl.ds(32 * d, 32)]) for d in range(2)]
    l_o = [lcopy(og_ref.at[d], og.at[pl.ds(32 * d, 32)]) for d in range(2)]
    l_r = lcopy(rows_ref, rows)

    barrier = pltpu.get_barrier_semaphore()

    def greet(dev):
        pl.semaphore_signal(barrier, inc=1, device_id=dev, device_id_type=MESH)

    greet(partner)
    greet((t, other))
    for d in (1, -1, 2):
        greet(at_x(d))
    for d in (1, -1):
        greet(at_y(d))
        greet(at_z(d))
    for d in (1, 2, 3):
        greet((((zl + d) % 4) * 8 + y, s))

    win = pin_ref[...]
    gap = jnp.zeros((64, WIN - 448), BF16)

    @pl.when(t % 2 == 0)
    def _():
        ptall[t, :, :, :WIN] = jnp.concatenate([win, gap], axis=1).reshape(4, 16, WIN)

    @pl.when(t % 2 == 1)
    def _():
        ptall[t, :, :, :WIN] = jnp.concatenate([gap, win], axis=1).reshape(4, 16, WIN)

    ptall[t, :, :, WIN:] = pout_ref[...].reshape(4, 16, PW - WIN)
    pl.semaphore_wait(barrier, 12)

    half = pl.ds(2 * c, 2)

    def slot(dy, dz):
        return ((zl + 4 + dz) % 4) * 8 + (y + 8 + dy) % 8

    def psend(sl, rowsl, ss, rs, dev):
        ref = ptall.at[sl, rowsl]
        rcopy(ref, ref, ss, rs, dev).start()

    def pshare(sl, group=None):
        psend(sl, half, snd.at[S_PSH], one_r.at[R_PSH if group is None else group], partner)

    psend(t, half, snd.at[S_PZ], pz_r.at[0], at_z(1))
    psend(t, half, snd.at[S_PZ], pz_r.at[1], at_z(-1))

    def pwait(sem, n=2):
        drain(ptall.at[0, pl.ds(0, n)], sem)

    for k in (0, 2, 1, 3):
        for j in range(NSPLIT):
            dst = qall.at[s, k, j]
            rcopy(qsrc(k, j), dst, snd.at[S_X], xs_r.at[2, k, j], at_x(1)).start()
            rcopy(qsrc(k, j), dst, snd.at[S_X], xs_r.at[1, k, j], at_x(-1)).start()

    rcopy(prec_ref, rall.at[s], snd.at[S_RZ], one_r.at[R_RZ], (t, other)).start()
    for d in (1, -1, 2):
        rcopy(prec_ref, rall.at[s], snd.at[S_RX], one_r.at[R_RX], at_x(d)).start()

    def need(order, k, d):
        dy, dz = order[k]
        return 0 if dy == 0 else order.index((dy + d, dz)) + 1

    got = [0, 0]

    def yrecv_to(side, n):
        order, sems, d = ((UP, pyu_r, -1), (DN, pyd_r, 1))[side]
        while got[side] < n:
            k = got[side]
            pwait(sems.at[k])
            pshare(slot(order[k][0] + d, order[k][1]), R_PSH if k < 8 else R_PSH2)
            got[side] += 1

    def ysend(k):
        yrecv_to(0, need(UP, k, 1))
        psend(slot(*UP[k]), half, snd.at[S_PY], pyu_r.at[k], at_y(1))
        yrecv_to(1, need(DN, k, -1))
        psend(slot(*DN[k]), half, snd.at[S_PY], pyd_r.at[k], at_y(-1))

    def xorder(i):
        return i + i // 2 - 2 * (i // 3)

    def zchunk(n, group, up):
        xi, k, j = n // (2 * NSPLIT), (n // NSPLIT) % 2, n % NSPLIT
        sl = group * 8 + ((x + xorder(xi)) % 4) * 2 + c
        return qall.at[sl, k + (0 if up else 2), j]

    def qwait(i, k, j):
        if i == 0:
            pltpu.make_async_copy(qsrc(k, j), qall.at[s, k, j], xs_r.at[0, k, j]).wait()
        else:
            drain(qall.at[0, 0, 0], xs_r.at[i, k, j])

    def qshare(ref, group):
        rcopy(ref, ref, snd.at[S_QSH], one_r.at[group], partner).start()

    def own_group(xi, k, j):
        return qall.at[zh * 8 + ((x + [0, 1, 3, 2][xi]) % 4) * 2 + c, k, j]

    def zstep(tau):
        if tau < NZ:
            xi, k, j = tau // (2 * NSPLIT), (tau // NSPLIT) % 2, tau % NSPLIT
            for i in {0: (0,), 1: (1, 2), 2: (), 3: (3,)}[xi]:
                for kk in (k, k + 2):
                    qwait(i, kk, j)
                    qshare(own_group(i, kk, j), R_QSA)
            if xi == 1:
                lref = own_group(2, k, j)
                rcopy(lref, lref, snd.at[S_X], xs_r.at[3, k, j], at_x(1)).start()
                rref = own_group(1, k + 2, j)
                rcopy(rref, rref, snd.at[S_X], xs_r.at[3, k + 2, j], at_x(-1)).start()
        if tau < NZ:

            @pl.when(zl == 3)
            def _():
                ref = zchunk(tau, zh, True)
                rcopy(ref, ref, snd.at[S_Z], zu_r.at[tau], at_z(1)).start()

            @pl.when(zl == 0)
            def _():
                ref = zchunk(tau, zh, False)
                rcopy(ref, ref, snd.at[S_Z], zd_r.at[tau], at_z(-1)).start()

        u = tau - LAG * (zl + 1)

        @pl.when((u >= 0) & (u < NZ))
        def _():
            ref = zchunk(u, 1 - zh, True)
            drain(ref, zu_r.at[u])

            @pl.when(zl != 3)
            def _():
                rcopy(ref, ref, snd.at[S_Z], zu_r.at[u], at_z(1)).start()

            qshare(ref, R_QSB)

        v = tau - LAG * (4 - zl)

        @pl.when((v >= 0) & (v < NZ))
        def _():
            ref = zchunk(v, 1 - zh, False)
            drain(ref, zd_r.at[v])

            @pl.when(zl != 0)
            def _():
                rcopy(ref, ref, snd.at[S_Z], zd_r.at[v], at_z(-1)).start()

            qshare(ref, R_QSB)

    nsteps = NZ + 4 * LAG
    zs = iter(range(nsteps))

    def zrun(n):
        for _ in range(n):
            tau = next(zs, None)
            if tau is None:
                return
            zstep(tau)

    def score(group):
        @pl.loop(0, 4)
        def _(k):
            sl = group * 8 + 2 * k
            raw = jnp.zeros((128, 128), F32)
            for j in range(NSPLIT):
                blk = jnp.concatenate([qall[sl + h, i, j] for h in range(2) for i in range(4)], axis=0)
                raw = raw + nt_dot(blk, rowsb[:, ZCOLS * j : ZCOLS * (j + 1)])
            for h in range(2):
                w = plan_ref[sl + h].astype(F32)
                scores_ref[pl.ds(pl.multiple_of(64 * (sl + h), 64), 64), :] = raw[64 * h : 64 * h + 64] * w

    ysend(0)
    pwait(pz_r.at[0])
    psend(slot(0, -1), pl.ds(2 * c, 1), snd.at[S_PZH], pz_r.at[2], at_z(1))
    pwait(pz_r.at[1])
    psend(slot(0, 1), pl.ds(2 * c + 1, 1), snd.at[S_PZH], pz_r.at[3], at_z(-1))
    ysend(1)
    ysend(2)
    pshare(slot(0, -1))
    pshare(slot(0, 1))
    pwait(pz_r.at[2], 1)
    pwait(pz_r.at[3], 1)
    ysend(3)
    zrun(2)
    pshare(slot(0, 2))
    for k in range(4, NY):
        ysend(k)
        zrun(PLAN_Y)
    drain(rall.at[0], one_r.at[R_RZ])
    for d in (1, -1, 2):
        rcopy(rall.at[other], rall.at[other], snd.at[S_RX2], one_r.at[R_RX2], at_x(d)).start()
    l_r.wait()
    rowsb[...] = rows[...].astype(BF16)
    for cp in l_a + l_o:
        cp.wait()

    def project(acc, dys):
        left, right = acc
        for dy in dys:
            for dz in (0, 1, 2, 3):
                i = slot(dy, dz)
                start = pl.multiple_of(448 * i - 64 * (i % 2), 128)
                w = ptall[i].reshape(64, PW)
                left = left + nt_dot(act[:, pl.ds(start, WIN)], w[:, :WIN])
                right = right + nt_dot(w[:, WIN:], og[:, pl.ds(pl.multiple_of(128 * i, 128), 128)])
        return left, right

    drain(ptall.at[pl.ds(0, 19), pl.ds(0, 2)], one_r.at[R_PSH])
    zrun(1)
    acc = project((jnp.zeros((64, 64), F32), jnp.zeros((64, 64), F32)), (0, -1, 1, -2, 2))
    yrecv_to(0, NY)
    yrecv_to(1, NY)
    zrun(1)
    drain(rall.at[pl.ds(0, 3)], one_r.at[R_RX])
    drain(ptall.at[pl.ds(0, 12), pl.ds(0, 2)], one_r.at[R_PSH2])
    left, right = project(acc, (-3, 3, 4))
    left = left.astype(BF16)
    right = right.astype(BF16)
    r0 = lax.broadcasted_iota(jnp.int32, (64, 64), 0)
    r1 = lax.broadcasted_iota(jnp.int32, (64, 64), 1)
    pick = (r1 == 2 * (r0 % 32) + r0 // 32).astype(F32).astype(BF16)
    right = jnp.dot(pick, right, preferred_element_type=F32)
    for d in range(2):
        live = valid_ref[pl.ds(d, 1), :].astype(F32)
        rest = jnp.zeros((1, 32), F32)
        masked = (right * jnp.concatenate([live, rest] if d == 0 else [rest, live], axis=1)).astype(BF16)
        outer = jnp.dot(masked, left, preferred_element_type=F32)
        part[:, d, :] = jnp.concatenate([outer[:32], outer[32:]], axis=1)

    l_pr.wait()
    drain(rall.at[pl.ds(0, 3)], one_r.at[R_RX2])

    @pl.loop(0, 8)
    def _(k):
        ref = rall.at[2 * k + c]
        rcopy(ref, ref, snd.at[S_RSH], one_r.at[R_RSH], partner).start()

    @pl.loop(1, NT)
    def _(k):
        to = (t + k) % NT
        rcopy(part.at[to], rsbuf.at[t], snd.at[S_RS], one_r.at[R_RS], (to, s)).start()

    rsbuf[t] = part[t]
    zrun(PLAN_RS)
    drain(rall.at[pl.ds(0, 8)], one_r.at[R_RSH])
    prows = rall[...].astype(F32).reshape(128, 4096).astype(BF16)
    own_q = jnp.concatenate(
        [jnp.concatenate([qall[s, k, j] for j in range(NSPLIT)], axis=1) for k in range(4)], axis=0
    )
    qp = nt_dot(own_q, prows).astype(BF16)
    drain(rsbuf.at[pl.ds(0, NT - 1)], one_r.at[R_RS])
    total = jnp.sum(rsbuf[...], axis=0) * (1.0 / 32.0)
    gown[...] = total.astype(BF16).astype(F32)
    gt[t] = gown[...]
    gs[s] = gown[...]

    @pl.loop(1, NS)
    def _(k):
        rcopy(gown, gs.at[s], snd.at[S_GS], one_r.at[R_GS], (t, (s + k) % NS)).start()

    @pl.loop(1, NT)
    def _(k):
        rcopy(gown, gt.at[t], snd.at[S_GT], one_r.at[R_GT], ((t + k) % NT, s)).start()

    zrun(PLAN_AG)
    drain(gs.at[pl.ds(0, NS - 1)], one_r.at[R_GS])
    docs = jnp.concatenate([gs[:, 0, :], gs[:, 1, :]], axis=0)
    acc = jnp.zeros((16, 128), F32)
    d0 = lax.broadcasted_iota(jnp.int32, (16, 32), 0)
    d1 = lax.broadcasted_iota(jnp.int32, (16, 32), 1)
    none = jnp.zeros((64, 128), BF16)
    for h in range(2):
        put = (d0 + 16 * h == 2 * (d1 % 16) + d1 // 16).astype(F32).astype(BF16)
        block = jnp.dot(put, docs.astype(BF16), preferred_element_type=F32).astype(BF16)
        acc = acc + nt_dot(block, jnp.concatenate([qp, none] if h == 0 else [none, qp], axis=0))
    arsrc[...] = acc
    ary[y] = acc

    @pl.loop(1, 8)
    def _(k):
        rcopy(arsrc, ary.at[y], snd.at[S_ARY], one_r.at[R_ARY], at_y(k)).start()

    zrun(PLAN_AR)
    drain(gt.at[pl.ds(0, NT - 1)], one_r.at[R_GT])
    pdoc_ref[...] = nt_dot(jnp.concatenate([gt[i] for i in range(NT)], axis=1).astype(BF16), prows)

    drain(ary.at[pl.ds(0, 7)], one_r.at[R_ARY])
    acc = jnp.sum(ary[...], axis=0)
    arsrc2[...] = acc
    arz[zl] = acc

    @pl.loop(1, 4)
    def _(k):
        rcopy(arsrc2, arz.at[zl], snd.at[S_ARZ], one_r.at[R_ARZ], (((zl + k) % 4) * 8 + y, s)).start()

    drain(qall.at[pl.ds(0, 4)], one_r.at[R_QSA])
    score(zh)
    zrun(nsteps)
    drain(qall.at[pl.ds(0, 4)], one_r.at[R_QSB])
    score(1 - zh)

    drain(arz.at[pl.ds(0, 3)], one_r.at[R_ARZ])
    acc = jnp.sum(arz[...], axis=0)
    dsc_ref[...] = jnp.concatenate([acc[:, :64], acc[:, 64:]], axis=0)

    sent(ptall.at[pl.ds(0, 2), pl.ds(0, 2)], snd.at[S_PZ])
    sent(ptall.at[0, pl.ds(0, 2)], snd.at[S_PZH])
    sent(ptall.at[pl.ds(0, 2 * NY), pl.ds(0, 2)], snd.at[S_PY])
    sent(ptall.at[pl.ds(0, NT - 1), pl.ds(0, 2)], snd.at[S_PSH])
    sent(qall.at[pl.ds(0, 3)], snd.at[S_X])
    sent(qall.at[pl.ds(0, 4)], snd.at[S_Z])
    sent(qall.at[pl.ds(0, 8)], snd.at[S_QSH])
    sent(rall.at[0], snd.at[S_RZ])
    sent(rall.at[pl.ds(0, 3)], snd.at[S_RX])
    sent(rall.at[pl.ds(0, 3)], snd.at[S_RX2])
    sent(rall.at[pl.ds(0, 8)], snd.at[S_RSH])
    sent(rsbuf.at[pl.ds(0, NT - 1)], snd.at[S_RS])
    sent(gt.at[pl.ds(0, NT - 1)], snd.at[S_GT])
    sent(gs.at[pl.ds(0, NS - 1)], snd.at[S_GS])
    sent(ary.at[pl.ds(0, 7)], snd.at[S_ARY])
    sent(arz.at[pl.ds(0, 3)], snd.at[S_ARZ])


def hand_over(a_ref, b_ref, c_ref, a_out, b_out, c_out):
    a_out[...] = a_ref[...]
    b_out[...] = b_ref[...]
    c_out[...] = c_ref[...]


def local(activations, out_grads, validity, proj_in, proj_out, precond, queries, store_rows, plan):
    hbm = pl.BlockSpec(memory_space=pl.ANY)
    vm = pl.BlockSpec(memory_space=pltpu.VMEM)
    sm = pl.BlockSpec(memory_space=pltpu.SMEM)
    dma = pltpu.SemaphoreType.DMA
    made = pl.pallas_call(
        kernel,
        out_shape=(
            jax.ShapeDtypeStruct((1024, 128), F32),
            jax.ShapeDtypeStruct((2, 128), F32),
            jax.ShapeDtypeStruct((32, 64), F32),
        ),
        in_specs=[sm, vm, vm, vm, hbm, hbm, hbm, hbm, hbm],
        out_specs=(vm, vm, vm),
        scratch_shapes=[
            pltpu.VMEM((NT, 4, 16, PW), BF16),
            pltpu.VMEM((64, 14336), BF16),
            pltpu.VMEM((64, 4096), BF16),
            pltpu.VMEM((128, 4096), F32),
            pltpu.VMEM((128, 4096), BF16),
            pltpu.VMEM((NS, 4, NSPLIT, 16, ZCOLS), BF16),
            pltpu.VMEM((NS, 8, 4096), BF16),
            pltpu.VMEM((NT, 2, 128), F32),
            pltpu.VMEM((NT, 2, 128), F32),
            pltpu.VMEM((2, 128), F32),
            pltpu.VMEM((NT, 2, 128), F32),
            pltpu.VMEM((NS, 2, 128), F32),
            pltpu.VMEM((8, 16, 128), F32),
            pltpu.VMEM((4, 16, 128), F32),
            pltpu.VMEM((16, 128), F32),
            pltpu.VMEM((16, 128), F32),
            dma((6,)),
            dma((4,)),
            dma((NY,)),
            dma((NY,)),
            dma((4, 4, NSPLIT)),
            dma((NZ,)),
            dma((NZ,)),
            dma((13,)),
            dma((16,)),
        ],
        compiler_params=pltpu.CompilerParams(collective_id=0, has_side_effects=True),
        name="logra",
    )(
        plan.reshape(16),
        validity,
        proj_in.T,
        proj_out.T,
        activations,
        out_grads,
        precond,
        queries.reshape(4, 16, 4096),
        store_rows,
    )
    scores, precond_docs, doc_scores = pl.pallas_call(
        hand_over,
        out_shape=tuple(jax.ShapeDtypeStruct(m.shape, m.dtype) for m in made),
        in_specs=[vm] * 3,
        out_specs=(vm,) * 3,
        name="hand_over",
    )(*made)
    return scores, precond_docs, doc_scores.T


def solution(mesh):
    return jax.shard_map(
        local,
        mesh=mesh,
        in_specs=(
            P("store", "tok", None),
            P("store", "tok", None),
            P("store", "tok"),
            P("tok", None),
            P("tok", None),
            P(("tok", "store"), None),
            P("store", None),
            P(("tok", "store"), None),
            P(None, ("tok", "store")),
        ),
        out_specs=(P(None, ("tok", "store")), P("store", "tok"), P("store", None)),
        check_vma=False,
    )
```

```python
import functools
import math

import jax
import jax.numpy as jnp
from jax import lax
from jax.experimental import pallas as pl
from jax.experimental.pallas import tpu as pltpu
from jax.sharding import PartitionSpec as P

MESH = pl.DeviceIdType.MESH
NT, NS = 32, 16
WIN = 512
PW = 640
QCOLS = 4096
F32 = jnp.float32
BF16 = jnp.bfloat16

UP = [(0, 0), (0, -1), (0, 1), (0, 2)] + [(-k, d) for k in (1, 2) for d in (0, -1, 1, 2)] + [(-3, 0), (-3, -1)]
DN = [(0, 0), (0, 1), (0, -1), (0, 2)] + [(k, d) for k in (1, 2) for d in (0, 1, -1, 2)] + [(3, 1), (3, 2)]
NY = len(UP)
DYS = (0, -1, 1, -2, 2, -3, 3, 4)
NSPLIT = 2
NZ = 8 * NSPLIT
ZCOLS = QCOLS // NSPLIT
LAG = 3
PLAN_Y = 1
PLAN_RS = 3
PLAN_AG = 4
PLAN_AR = 3


def nt_dot(a, b):
    return lax.dot_general(a, b, (((1,), (1,)), ((), ())), preferred_element_type=F32)


def kernel(
    plan_ref, valid_ref, pin_ref, pout_ref, act_ref, og_ref, prec_ref, q_ref, rows_ref,
    scores_ref, pdoc_ref, dsc_ref,
    ptall, act, og, rows, rowsb, qall, rall, part, rsbuf, gown, gt, gs, ary, arz, arsrc, arsrc2,
    lsem, pz_r, pb_r, pyu_r, pyd_r, xs_r, zu_r, zd_r, one_r, snd,
):
    t = lax.axis_index("tok")
    s = lax.axis_index("store")
    zl, y = t // 8, t % 8
    zh, x, c = s // 8, (s // 2) % 4, s % 2
    z = zh * 4 + zl

    def at_z(d):
        zz = (z + 8 + d) % 8
        return ((zz % 4) * 8 + y, (zz // 4) * 8 + x * 2 + c)

    def at_y(d):
        return (zl * 8 + (y + 8 + d) % 8, s)

    def at_x(d):
        return (t, zh * 8 + ((x + 4 + d) % 4) * 2 + c)

    partner = (t, zh * 8 + x * 2 + (1 - c))
    other = (1 - zh) * 8 + x * 2 + c

    def rcopy(src, dst, ss, rs, dev):
        return pltpu.make_async_remote_copy(
            src_ref=src, dst_ref=dst, send_sem=ss, recv_sem=rs, device_id=dev, device_id_type=MESH
        )

    def drain(ref, sem):
        rcopy(ref, ref, snd.at[0], sem, partner).wait_recv()

    def sent(ref, sem):
        rcopy(ref, ref, sem, one_r.at[0], partner).wait_send()

    def qsrc(k, j):
        return q_ref.at[k, :, pl.ds(j * ZCOLS, ZCOLS)]

    R_PSH, R_PSH2, R_QSA, R_QSB, R_RZ, R_RX, R_RX2, R_RSH, R_RS, R_GT, R_GS, R_ARY, R_ARZ = range(13)
    (S_PZ, S_PZH, S_PY, S_PSH, S_X, S_Z, S_QSH, S_RZ, S_RX, S_RX2, S_RSH, S_RS, S_GT, S_GS, S_ARY, S_ARZ, S_PB) = range(17)

    loc = []

    def lcopy(src, dst):
        cp = pltpu.make_async_copy(src, dst, lsem.at[len(loc)])
        cp.start()
        loc.append(cp)
        return cp

    l_pr = lcopy(prec_ref, rall.at[s])
    for k in range(4):
        for j in range(NSPLIT):
            pltpu.make_async_copy(qsrc(k, j), qall.at[s, k, j], xs_r.at[0, k, j]).start()
    l_a = [lcopy(act_ref.at[d], act.at[pl.ds(32 * d, 32)]) for d in range(2)]
    l_o = [lcopy(og_ref.at[d], og.at[pl.ds(32 * d, 32)]) for d in range(2)]
    l_r = lcopy(rows_ref, rows)

    barrier = pltpu.get_barrier_semaphore()

    def greet(dev):
        pl.semaphore_signal(barrier, inc=1, device_id=dev, device_id_type=MESH)

    greet(partner)
    greet((t, other))
    for d in (1, -1, 2):
        greet(at_x(d))
    for d in (1, -1):
        greet(at_y(d))
        greet(at_z(d))
    for d in (1, 2, 3):
        greet((((zl + d) % 4) * 8 + y, s))

    win = pin_ref[...]
    gap = jnp.zeros((64, WIN - 448), BF16)

    @pl.when(t % 2 == 0)
    def _():
        ptall[t, :, :, :WIN] = jnp.concatenate([win, gap], axis=1).reshape(4, 16, WIN)

    @pl.when(t % 2 == 1)
    def _():
        ptall[t, :, :, :WIN] = jnp.concatenate([gap, win], axis=1).reshape(4, 16, WIN)

    ptall[t, :, :, WIN:] = pout_ref[...].reshape(4, 16, PW - WIN)
    pl.semaphore_wait(barrier, 12)

    qa, qb = pl.ds(2 * c, 1), pl.ds(2 * c + 1, 1)

    def slot(dy, dz):
        return ((zl + 4 + dz) % 4) * 8 + (y + 8 + dy) % 8

    def psend(sl, rowsl, ss, rs, dev):
        ref = ptall.at[sl, rowsl]
        rcopy(ref, ref, ss, rs, dev).start()

    def pshare(dy, dz, q):
        psend(slot(dy, dz), q, snd.at[S_PSH], one_r.at[R_PSH if abs(dy) <= 2 else R_PSH2], partner)

    def pwait(sem):
        drain(ptall.at[0, pl.ds(0, 1)], sem)

    def bsend(dy, dz, n, dev):
        psend(slot(dy, dz), qb, snd.at[S_PB], pb_r.at[n], dev)

    def bz_send(i):
        bsend(DYS[i], 0, 7 + i, at_z(1))
        bsend(DYS[i], 0, 15 + i, at_z(-1))

    def bz_recv(i):
        pwait(pb_r.at[7 + i])
        if i % 2 == 0:
            bsend(DYS[i], -1, 23 + i, at_z(1))
        pwait(pb_r.at[15 + i])
        if i % 2 == 1:
            bsend(DYS[i], 1, 23 + i, at_z(-1))
        pshare(DYS[i], -1, qb)
        pshare(DYS[i], 1, qb)

    def bz_fin(i):
        pwait(pb_r.at[23 + i])
        pshare(DYS[i], 2, qb)

    def by_recv(r):
        pwait(pb_r.at[r - 1])
        if r <= 3:
            bsend(-r, 0, r, at_y(1))
            pwait(pb_r.at[3 + r])
            if r <= 2:
                bsend(r, 0, 4 + r, at_y(-1))
        for i in {1: (1, 2), 2: (3, 4), 3: (5, 6), 4: (7,)}[r]:
            bz_send(i)
            pshare(DYS[i], 0, qb)

    got = set()

    def yrecv(side, k):
        if (side, k) in got:
            return
        got.add((side, k))
        order, sems, d = ((UP, pyu_r, -1), (DN, pyd_r, 1))[side]
        pwait(sems.at[k])
        pshare(order[k][0] + d, order[k][1], qa)

    def usend(*ks):
        for k in ks:
            dy, dz = UP[k]
            if dy:
                yrecv(0, UP.index((dy + 1, dz)))
            psend(slot(dy, dz), qa, snd.at[S_PY], pyu_r.at[k], at_y(1))

    def dsend(*ks):
        for k in ks:
            dy, dz = DN[k]
            if dy:
                yrecv(1, DN.index((dy - 1, dz)))
            psend(slot(dy, dz), qa, snd.at[S_PY], pyd_r.at[k], at_y(-1))

    def both(*ks):
        for k in ks:
            usend(k)
            dsend(k)

    psend(t, qa, snd.at[S_PZ], pz_r.at[0], at_z(1))
    psend(t, qa, snd.at[S_PZ], pz_r.at[1], at_z(-1))
    bsend(0, 0, 0, at_y(1))
    bsend(0, 0, 4, at_y(-1))
    both(0)
    bz_send(0)

    for k in (0, 2, 1, 3):
        for j in range(NSPLIT):
            dst = qall.at[s, k, j]
            rcopy(qsrc(k, j), dst, snd.at[S_X], xs_r.at[2, k, j], at_x(1)).start()
            rcopy(qsrc(k, j), dst, snd.at[S_X], xs_r.at[1, k, j], at_x(-1)).start()

    rcopy(prec_ref, rall.at[s], snd.at[S_RZ], one_r.at[R_RZ], (t, other)).start()
    for d in (1, -1, 2):
        rcopy(prec_ref, rall.at[s], snd.at[S_RX], one_r.at[R_RX], at_x(d)).start()

    def xorder(i):
        return i + i // 2 - 2 * (i // 3)

    def zchunk(n, group, up):
        xi, k, j = n // (2 * NSPLIT), (n // NSPLIT) % 2, n % NSPLIT
        sl = group * 8 + ((x + xorder(xi)) % 4) * 2 + c
        return qall.at[sl, k + (0 if up else 2), j]

    def qwait(i, k, j):
        if i == 0:
            pltpu.make_async_copy(qsrc(k, j), qall.at[s, k, j], xs_r.at[0, k, j]).wait()
        else:
            drain(qall.at[0, 0, 0], xs_r.at[i, k, j])

    def qshare(ref, group):
        rcopy(ref, ref, snd.at[S_QSH], one_r.at[group], partner).start()

    def own_group(xi, k, j):
        return qall.at[zh * 8 + ((x + [0, 1, 3, 2][xi]) % 4) * 2 + c, k, j]

    def zstep(tau):
        if tau < NZ:
            xi, k, j = tau // (2 * NSPLIT), (tau // NSPLIT) % 2, tau % NSPLIT
            for i in {0: (0,), 1: (1, 2), 2: (), 3: (3,)}[xi]:
                for kk in (k, k + 2):
                    qwait(i, kk, j)
                    qshare(own_group(i, kk, j), R_QSA)
            if xi == 1:
                lref = own_group(2, k, j)
                rcopy(lref, lref, snd.at[S_X], xs_r.at[3, k, j], at_x(1)).start()
                rref = own_group(1, k + 2, j)
                rcopy(rref, rref, snd.at[S_X], xs_r.at[3, k + 2, j], at_x(-1)).start()
        if tau < NZ:

            @pl.when(zl == 3)
            def _():
                ref = zchunk(tau, zh, True)
                rcopy(ref, ref, snd.at[S_Z], zu_r.at[tau], at_z(1)).start()

            @pl.when(zl == 0)
            def _():
                ref = zchunk(tau, zh, False)
                rcopy(ref, ref, snd.at[S_Z], zd_r.at[tau], at_z(-1)).start()

        u = tau - LAG * (zl + 1)

        @pl.when((u >= 0) & (u < NZ))
        def _():
            ref = zchunk(u, 1 - zh, True)
            drain(ref, zu_r.at[u])

            @pl.when(zl != 3)
            def _():
                rcopy(ref, ref, snd.at[S_Z], zu_r.at[u], at_z(1)).start()

            qshare(ref, R_QSB)

        v = tau - LAG * (4 - zl)

        @pl.when((v >= 0) & (v < NZ))
        def _():
            ref = zchunk(v, 1 - zh, False)
            drain(ref, zd_r.at[v])

            @pl.when(zl != 0)
            def _():
                rcopy(ref, ref, snd.at[S_Z], zd_r.at[v], at_z(-1)).start()

            qshare(ref, R_QSB)

    nsteps = NZ + 4 * LAG
    zs = iter(range(nsteps))

    def zrun(n):
        for _ in range(n):
            tau = next(zs, None)
            if tau is None:
                return
            zstep(tau)

    def score(group):
        @pl.loop(0, 4)
        def _(k):
            sl = group * 8 + 2 * k
            raw = jnp.zeros((128, 128), F32)
            for j in range(NSPLIT):
                blk = jnp.concatenate([qall[sl + h, i, j] for h in range(2) for i in range(4)], axis=0)
                raw = raw + nt_dot(blk, rowsb[:, ZCOLS * j : ZCOLS * (j + 1)])
            for h in range(2):
                w = plan_ref[sl + h].astype(F32)
                scores_ref[pl.ds(pl.multiple_of(64 * (sl + h), 64), 64), :] = raw[64 * h : 64 * h + 64] * w

    pwait(pz_r.at[0])
    psend(slot(0, -1), qa, snd.at[S_PZH], pz_r.at[2], at_z(1))
    pwait(pz_r.at[1])
    both(1, 2)
    by_recv(1)
    both(4)
    pshare(0, -1, qa)
    pshare(0, 1, qa)
    bz_recv(0)
    zrun(2)
    pwait(pz_r.at[2])
    both(3)
    by_recv(2)
    both(5, 6, 8)
    pshare(0, 2, qa)
    for i in (1, 2):
        bz_recv(i)
    bz_fin(0)
    zrun(3)
    by_recv(3)
    both(7, 9, 10)
    usend(12)
    for i in (3, 4):
        bz_recv(i)
    for i in (1, 2):
        bz_fin(i)
    zrun(3)
    by_recv(4)
    both(11)
    usend(13)
    dsend(12)
    for i in (5, 6):
        bz_recv(i)
    for i in (3, 4):
        bz_fin(i)
    zrun(3)
    dsend(13)
    bz_recv(7)
    for k in range(8):
        yrecv(0, k)
        yrecv(1, k)
    drain(rall.at[0], one_r.at[R_RZ])
    for d in (1, -1, 2):
        rcopy(rall.at[other], rall.at[other], snd.at[S_RX2], one_r.at[R_RX2], at_x(d)).start()
    l_r.wait()
    rowsb[...] = rows[...].astype(BF16)
    for cp in l_a + l_o:
        cp.wait()

    def project(acc, dys):
        left, right = acc
        for dy in dys:
            for dz in (0, 1, 2, 3):
                i = slot(dy, dz)
                start = pl.multiple_of(448 * i - 64 * (i % 2), 128)
                w = ptall[i].reshape(64, PW)
                left = left + nt_dot(act[:, pl.ds(start, WIN)], w[:, :WIN])
                right = right + nt_dot(w[:, WIN:], og[:, pl.ds(pl.multiple_of(128 * i, 128), 128)])
        return left, right

    drain(ptall.at[pl.ds(0, 19), pl.ds(0, 2)], one_r.at[R_PSH])
    zrun(2)
    acc = project((jnp.zeros((64, 64), F32), jnp.zeros((64, 64), F32)), (0, -1, 1, -2, 2))
    for i in (5, 6, 7):
        bz_fin(i)
    for k in range(NY):
        yrecv(0, k)
        yrecv(1, k)
    zrun(1)
    drain(rall.at[pl.ds(0, 3)], one_r.at[R_RX])
    drain(ptall.at[pl.ds(0, 12), pl.ds(0, 2)], one_r.at[R_PSH2])
    left, right = project(acc, (-3, 3, 4))
    left = left.astype(BF16)
    right = right.astype(BF16)
    r0 = lax.broadcasted_iota(jnp.int32, (64, 64), 0)
    r1 = lax.broadcasted_iota(jnp.int32, (64, 64), 1)
    pick = (r1 == 2 * (r0 % 32) + r0 // 32).astype(F32).astype(BF16)
    right = jnp.dot(pick, right, preferred_element_type=F32)
    for d in range(2):
        live = valid_ref[pl.ds(d, 1), :].astype(F32)
        rest = jnp.zeros((1, 32), F32)
        masked = (right * jnp.concatenate([live, rest] if d == 0 else [rest, live], axis=1)).astype(BF16)
        outer = jnp.dot(masked, left, preferred_element_type=F32)
        part[:, d, :] = jnp.concatenate([outer[:32], outer[32:]], axis=1)

    l_pr.wait()
    drain(rall.at[pl.ds(0, 3)], one_r.at[R_RX2])

    @pl.loop(0, 8)
    def _(k):
        ref = rall.at[2 * k + c]
        rcopy(ref, ref, snd.at[S_RSH], one_r.at[R_RSH], partner).start()

    @pl.loop(1, NT)
    def _(k):
        to = (t + k) % NT
        rcopy(part.at[to], rsbuf.at[t], snd.at[S_RS], one_r.at[R_RS], (to, s)).start()

    rsbuf[t] = part[t]
    zrun(PLAN_RS)
    drain(rall.at[pl.ds(0, 8)], one_r.at[R_RSH])
    prows = rall[...].astype(F32).reshape(128, 4096).astype(BF16)
    own_q = jnp.concatenate(
        [jnp.concatenate([qall[s, k, j] for j in range(NSPLIT)], axis=1) for k in range(4)], axis=0
    )
    qp = nt_dot(own_q, prows).astype(BF16)
    drain(rsbuf.at[pl.ds(0, NT - 1)], one_r.at[R_RS])
    total = jnp.sum(rsbuf[...], axis=0) * (1.0 / 32.0)
    gown[...] = total.astype(BF16).astype(F32)
    gt[t] = gown[...]
    gs[s] = gown[...]

    @pl.loop(1, NS)
    def _(k):
        rcopy(gown, gs.at[s], snd.at[S_GS], one_r.at[R_GS], (t, (s + k) % NS)).start()

    @pl.loop(1, NT)
    def _(k):
        rcopy(gown, gt.at[t], snd.at[S_GT], one_r.at[R_GT], ((t + k) % NT, s)).start()

    zrun(PLAN_AG)
    drain(gs.at[pl.ds(0, NS - 1)], one_r.at[R_GS])
    docs = jnp.concatenate([gs[:, 0, :], gs[:, 1, :]], axis=0)
    acc = jnp.zeros((16, 128), F32)
    d0 = lax.broadcasted_iota(jnp.int32, (16, 32), 0)
    d1 = lax.broadcasted_iota(jnp.int32, (16, 32), 1)
    none = jnp.zeros((64, 128), BF16)
    for h in range(2):
        put = (d0 + 16 * h == 2 * (d1 % 16) + d1 // 16).astype(F32).astype(BF16)
        block = jnp.dot(put, docs.astype(BF16), preferred_element_type=F32).astype(BF16)
        acc = acc + nt_dot(block, jnp.concatenate([qp, none] if h == 0 else [none, qp], axis=0))
    arsrc[...] = acc
    ary[y] = acc

    @pl.loop(1, 8)
    def _(k):
        rcopy(arsrc, ary.at[y], snd.at[S_ARY], one_r.at[R_ARY], at_y(k)).start()

    zrun(PLAN_AR)
    drain(gt.at[pl.ds(0, NT - 1)], one_r.at[R_GT])
    pdoc_ref[...] = nt_dot(jnp.concatenate([gt[i] for i in range(NT)], axis=1).astype(BF16), prows)

    drain(ary.at[pl.ds(0, 7)], one_r.at[R_ARY])
    acc = jnp.sum(ary[...], axis=0)
    arsrc2[...] = acc
    arz[zl] = acc

    @pl.loop(1, 4)
    def _(k):
        rcopy(arsrc2, arz.at[zl], snd.at[S_ARZ], one_r.at[R_ARZ], (((zl + k) % 4) * 8 + y, s)).start()

    drain(qall.at[pl.ds(0, 4)], one_r.at[R_QSA])
    score(zh)
    zrun(nsteps)
    drain(qall.at[pl.ds(0, 4)], one_r.at[R_QSB])
    score(1 - zh)

    drain(arz.at[pl.ds(0, 3)], one_r.at[R_ARZ])
    acc = jnp.sum(arz[...], axis=0)
    dsc_ref[...] = jnp.concatenate([acc[:, :64], acc[:, 64:]], axis=0)

    sent(ptall.at[0, pl.ds(0, 2)], snd.at[S_PZ])
    sent(ptall.at[0, pl.ds(0, 1)], snd.at[S_PZH])
    sent(ptall.at[pl.ds(0, NY), pl.ds(0, 2)], snd.at[S_PY])
    sent(ptall.at[pl.ds(0, 31), pl.ds(0, 1)], snd.at[S_PB])
    sent(ptall.at[pl.ds(0, NT - 1), pl.ds(0, 2)], snd.at[S_PSH])
    sent(qall.at[pl.ds(0, 3)], snd.at[S_X])
    sent(qall.at[pl.ds(0, 4)], snd.at[S_Z])
    sent(qall.at[pl.ds(0, 8)], snd.at[S_QSH])
    sent(rall.at[0], snd.at[S_RZ])
    sent(rall.at[pl.ds(0, 3)], snd.at[S_RX])
    sent(rall.at[pl.ds(0, 3)], snd.at[S_RX2])
    sent(rall.at[pl.ds(0, 8)], snd.at[S_RSH])
    sent(rsbuf.at[pl.ds(0, NT - 1)], snd.at[S_RS])
    sent(gt.at[pl.ds(0, NT - 1)], snd.at[S_GT])
    sent(gs.at[pl.ds(0, NS - 1)], snd.at[S_GS])
    sent(ary.at[pl.ds(0, 7)], snd.at[S_ARY])
    sent(arz.at[pl.ds(0, 3)], snd.at[S_ARZ])


def hand_over(a_ref, b_ref, c_ref, a_out, b_out, c_out):
    a_out[...] = a_ref[...]
    b_out[...] = b_ref[...]
    c_out[...] = c_ref[...]


def local(activations, out_grads, validity, proj_in, proj_out, precond, queries, store_rows, plan):
    hbm = pl.BlockSpec(memory_space=pl.ANY)
    vm = pl.BlockSpec(memory_space=pltpu.VMEM)
    sm = pl.BlockSpec(memory_space=pltpu.SMEM)
    dma = pltpu.SemaphoreType.DMA
    made = pl.pallas_call(
        kernel,
        out_shape=(
            jax.ShapeDtypeStruct((1024, 128), F32),
            jax.ShapeDtypeStruct((2, 128), F32),
            jax.ShapeDtypeStruct((32, 64), F32),
        ),
        in_specs=[sm, vm, vm, vm, hbm, hbm, hbm, hbm, hbm],
        out_specs=(vm, vm, vm),
        scratch_shapes=[
            pltpu.VMEM((NT, 4, 16, PW), BF16),
            pltpu.VMEM((64, 14336), BF16),
            pltpu.VMEM((64, 4096), BF16),
            pltpu.VMEM((128, 4096), F32),
            pltpu.VMEM((128, 4096), BF16),
            pltpu.VMEM((NS, 4, NSPLIT, 16, ZCOLS), BF16),
            pltpu.VMEM((NS, 8, 4096), BF16),
            pltpu.VMEM((NT, 2, 128), F32),
            pltpu.VMEM((NT, 2, 128), F32),
            pltpu.VMEM((2, 128), F32),
            pltpu.VMEM((NT, 2, 128), F32),
            pltpu.VMEM((NS, 2, 128), F32),
            pltpu.VMEM((8, 16, 128), F32),
            pltpu.VMEM((4, 16, 128), F32),
            pltpu.VMEM((16, 128), F32),
            pltpu.VMEM((16, 128), F32),
            dma((6,)),
            dma((3,)),
            dma((31,)),
            dma((NY,)),
            dma((NY,)),
            dma((4, 4, NSPLIT)),
            dma((NZ,)),
            dma((NZ,)),
            dma((13,)),
            dma((17,)),
        ],
        compiler_params=pltpu.CompilerParams(collective_id=0, has_side_effects=True),
        name="logra",
    )(
        plan.reshape(16),
        validity,
        proj_in.T,
        proj_out.T,
        activations,
        out_grads,
        precond,
        queries.reshape(4, 16, 4096),
        store_rows,
    )
    scores, precond_docs, doc_scores = pl.pallas_call(
        hand_over,
        out_shape=tuple(jax.ShapeDtypeStruct(m.shape, m.dtype) for m in made),
        in_specs=[vm] * 3,
        out_specs=(vm,) * 3,
        name="hand_over",
    )(*made)
    return scores, precond_docs, doc_scores.T


def solution(mesh):
    return jax.shard_map(
        local,
        mesh=mesh,
        in_specs=(
            P("store", "tok", None),
            P("store", "tok", None),
            P("store", "tok"),
            P("tok", None),
            P("tok", None),
            P(("tok", "store"), None),
            P("store", None),
            P(("tok", "store"), None),
            P(None, ("tok", "store")),
        ),
        out_specs=(P(None, ("tok", "store")), P("store", "tok"), P("store", None)),
        check_vma=False,
    )
```

```python
import functools
import math

import jax
import jax.numpy as jnp
from jax import lax
from jax.experimental import pallas as pl
from jax.experimental.pallas import tpu as pltpu
from jax.sharding import PartitionSpec as P

MESH = pl.DeviceIdType.MESH
NT, NS = 32, 16
WIN = 512
PW = 640
QCOLS = 4096
F32 = jnp.float32
BF16 = jnp.bfloat16

UP = [(0, 0), (0, -1), (0, 1), (0, 2)] + [(-k, d) for k in (1, 2) for d in (0, -1, 1, 2)] + [(-3, 0), (-3, -1)]
DN = [(0, 0), (0, 1), (0, -1), (0, 2)] + [(k, d) for k in (1, 2) for d in (0, 1, -1, 2)] + [(3, 1), (3, 2)]
NY = len(UP)
NSPLIT = 2
NZ = 6 * NSPLIT
ZCOLS = QCOLS // NSPLIT
LAG = 3
PLAN_Y = 1
PLAN_RS = 3
PLAN_AG = 4
PLAN_AR = 3


def nt_dot(a, b):
    return lax.dot_general(a, b, (((1,), (1,)), ((), ())), preferred_element_type=F32)


def kernel(
    plan_ref, valid_ref, pin_ref, pout_ref, act_ref, og_ref, prec_ref, q_ref, rows_ref,
    scores_ref, pdoc_ref, dsc_ref,
    ptall, act, og, rows, rowsb, qall, rall, part, rsbuf, gown, gt, gs, ary, arz, arsrc, arsrc2,
    lsem, pz_r, pyu_r, pyd_r, xs_r, zu_r, zd_r, xo_r, one_r, snd,
):
    t = lax.axis_index("tok")
    s = lax.axis_index("store")
    zl, y = t // 8, t % 8
    zh, x, c = s // 8, (s // 2) % 4, s % 2
    z = zh * 4 + zl

    def at_z(d):
        zz = (z + 8 + d) % 8
        return ((zz % 4) * 8 + y, (zz // 4) * 8 + x * 2 + c)

    def at_y(d):
        return (zl * 8 + (y + 8 + d) % 8, s)

    def at_x(d):
        return (t, zh * 8 + ((x + 4 + d) % 4) * 2 + c)

    partner = (t, zh * 8 + x * 2 + (1 - c))
    other = (1 - zh) * 8 + x * 2 + c

    def rcopy(src, dst, ss, rs, dev):
        return pltpu.make_async_remote_copy(
            src_ref=src, dst_ref=dst, send_sem=ss, recv_sem=rs, device_id=dev, device_id_type=MESH
        )

    def drain(ref, sem):
        rcopy(ref, ref, snd.at[0], sem, partner).wait_recv()

    def sent(ref, sem):
        rcopy(ref, ref, sem, one_r.at[0], partner).wait_send()

    def qsrc(k, j):
        return q_ref.at[k, :, pl.ds(j * ZCOLS, ZCOLS)]

    R_PSH, R_PSH2, R_QSA, R_QSB, R_RZ, R_RX, R_RX2, R_RSH, R_RS, R_GT, R_GS, R_ARY, R_ARZ = range(13)
    (S_PZ, S_PZH, S_PY, S_PSH, S_X, S_Z, S_QSH, S_RZ, S_RX, S_RX2, S_RSH, S_RS, S_GT, S_GS, S_ARY, S_ARZ) = range(16)

    loc = []

    def lcopy(src, dst):
        cp = pltpu.make_async_copy(src, dst, lsem.at[len(loc)])
        cp.start()
        loc.append(cp)
        return cp

    l_pr = lcopy(prec_ref, rall.at[s])
    for k in range(4):
        for j in range(NSPLIT):
            pltpu.make_async_copy(qsrc(k, j), qall.at[s, k, j], xs_r.at[0, k, j]).start()
    l_a = [lcopy(act_ref.at[d], act.at[pl.ds(32 * d, 32)]) for d in range(2)]
    l_o = [lcopy(og_ref.at[d], og.at[pl.ds(32 * d, 32)]) for d in range(2)]
    l_r = lcopy(rows_ref, rows)

    barrier = pltpu.get_barrier_semaphore()

    def greet(dev):
        pl.semaphore_signal(barrier, inc=1, device_id=dev, device_id_type=MESH)

    greet(partner)
    greet((t, other))
    for d in (1, -1, 2):
        greet(at_x(d))
    for d in (1, -1):
        greet(at_y(d))
        greet(at_z(d))
    for d in (1, 2, 3):
        greet((((zl + d) % 4) * 8 + y, s))

    win = pin_ref[...]
    gap = jnp.zeros((64, WIN - 448), BF16)

    @pl.when(t % 2 == 0)
    def _():
        ptall[t, :, :, :WIN] = jnp.concatenate([win, gap], axis=1).reshape(4, 16, WIN)

    @pl.when(t % 2 == 1)
    def _():
        ptall[t, :, :, :WIN] = jnp.concatenate([gap, win], axis=1).reshape(4, 16, WIN)

    ptall[t, :, :, WIN:] = pout_ref[...].reshape(4, 16, PW - WIN)
    pl.semaphore_wait(barrier, 12)

    half = pl.ds(2 * c, 2)

    def slot(dy, dz):
        return ((zl + 4 + dz) % 4) * 8 + (y + 8 + dy) % 8

    def psend(sl, rowsl, ss, rs, dev):
        ref = ptall.at[sl, rowsl]
        rcopy(ref, ref, ss, rs, dev).start()

    def pshare(sl, group=None):
        psend(sl, half, snd.at[S_PSH], one_r.at[R_PSH if group is None else group], partner)

    psend(t, half, snd.at[S_PZ], pz_r.at[0], at_z(1))
    psend(t, half, snd.at[S_PZ], pz_r.at[1], at_z(-1))

    def pwait(sem, n=2):
        drain(ptall.at[0, pl.ds(0, n)], sem)

    for k in (0, 2, 1, 3):
        for j in range(NSPLIT):
            dst = qall.at[s, k, j]
            rcopy(qsrc(k, j), dst, snd.at[S_X], xs_r.at[2, k, j], at_x(1)).start()
            rcopy(qsrc(k, j), dst, snd.at[S_X], xs_r.at[1, k, j], at_x(-1)).start()

    rcopy(prec_ref, rall.at[s], snd.at[S_RZ], one_r.at[R_RZ], (t, other)).start()
    for d in (1, -1, 2):
        rcopy(prec_ref, rall.at[s], snd.at[S_RX], one_r.at[R_RX], at_x(d)).start()

    def need(order, k, d):
        dy, dz = order[k]
        return 0 if dy == 0 else order.index((dy + d, dz)) + 1

    got = [0, 0]

    def yrecv_to(side, n):
        order, sems, d = ((UP, pyu_r, -1), (DN, pyd_r, 1))[side]
        while got[side] < n:
            k = got[side]
            pwait(sems.at[k])
            pshare(slot(order[k][0] + d, order[k][1]), R_PSH if k < 8 else R_PSH2)
            got[side] += 1

    def ysend(k):
        yrecv_to(0, need(UP, k, 1))
        psend(slot(*UP[k]), half, snd.at[S_PY], pyu_r.at[k], at_y(1))
        yrecv_to(1, need(DN, k, -1))
        psend(slot(*DN[k]), half, snd.at[S_PY], pyd_r.at[k], at_y(-1))

    def xorder(i):
        return i + i // 2 - 2 * (i // 3)

    def zchunk(n, group, up):
        xi, k, j = n // (2 * NSPLIT), (n // NSPLIT) % 2, n % NSPLIT
        sl = group * 8 + ((x + xorder(xi)) % 4) * 2 + c
        return qall.at[sl, k + (0 if up else 2), j]

    def qwait(i, k, j):
        if i == 0:
            pltpu.make_async_copy(qsrc(k, j), qall.at[s, k, j], xs_r.at[0, k, j]).wait()
        else:
            drain(qall.at[0, 0, 0], xs_r.at[i, k, j])

    def qshare(ref, group):
        rcopy(ref, ref, snd.at[S_QSH], one_r.at[group], partner).start()

    def own_group(xi, k, j):
        return qall.at[zh * 8 + ((x + [0, 1, 3, 2][xi]) % 4) * 2 + c, k, j]

    def zstep(tau):
        if tau < 8 * NSPLIT:
            xi, k, j = tau // (2 * NSPLIT), (tau // NSPLIT) % 2, tau % NSPLIT
            for i in {0: (0,), 1: (1, 2), 2: (), 3: (3,)}[xi]:
                for kk in (k, k + 2):
                    qwait(i, kk, j)
                    qshare(own_group(i, kk, j), R_QSA)
            if xi == 1:
                lref = own_group(2, k, j)
                rcopy(lref, lref, snd.at[S_X], xs_r.at[3, k, j], at_x(1)).start()
                rref = own_group(1, k + 2, j)
                rcopy(rref, rref, snd.at[S_X], xs_r.at[3, k + 2, j], at_x(-1)).start()
        if tau < NZ:

            @pl.when(zl == 3)
            def _():
                ref = zchunk(tau, zh, True)
                rcopy(ref, ref, snd.at[S_Z], zu_r.at[tau], at_z(1)).start()

            @pl.when(zl == 0)
            def _():
                ref = zchunk(tau, zh, False)
                rcopy(ref, ref, snd.at[S_Z], zd_r.at[tau], at_z(-1)).start()

        u = tau - LAG * (zl + 1)

        @pl.when((u >= 0) & (u < NZ))
        def _():
            ref = zchunk(u, 1 - zh, True)
            drain(ref, zu_r.at[u])

            @pl.when(zl != 3)
            def _():
                rcopy(ref, ref, snd.at[S_Z], zu_r.at[u], at_z(1)).start()

            qshare(ref, R_QSB)

            @pl.when((u >= 2 * NSPLIT) & (u < 4 * NSPLIT))
            def _():
                rcopy(ref, ref, snd.at[S_X], xo_r.at[u - 2 * NSPLIT], at_x(-1)).start()

        v = tau - LAG * (4 - zl)

        @pl.when((v >= 0) & (v < NZ))
        def _():
            ref = zchunk(v, 1 - zh, False)
            drain(ref, zd_r.at[v])

            @pl.when(zl != 0)
            def _():
                rcopy(ref, ref, snd.at[S_Z], zd_r.at[v], at_z(-1)).start()

            qshare(ref, R_QSB)

            @pl.when(v >= 4 * NSPLIT)
            def _():
                rcopy(ref, ref, snd.at[S_X], xo_r.at[v - 2 * NSPLIT], at_x(1)).start()

    nsteps = NZ + 4 * LAG
    zs = iter(range(nsteps))

    def zrun(n):
        for _ in range(n):
            tau = next(zs, None)
            if tau is None:
                return
            zstep(tau)

    def score(group):
        @pl.loop(0, 4)
        def _(k):
            sl = group * 8 + 2 * k
            raw = jnp.zeros((128, 128), F32)
            for j in range(NSPLIT):
                blk = jnp.concatenate([qall[sl + h, i, j] for h in range(2) for i in range(4)], axis=0)
                raw = raw + nt_dot(blk, rowsb[:, ZCOLS * j : ZCOLS * (j + 1)])
            for h in range(2):
                w = plan_ref[sl + h].astype(F32)
                scores_ref[pl.ds(pl.multiple_of(64 * (sl + h), 64), 64), :] = raw[64 * h : 64 * h + 64] * w

    ysend(0)
    pwait(pz_r.at[0])
    psend(slot(0, -1), pl.ds(2 * c, 1), snd.at[S_PZH], pz_r.at[2], at_z(1))
    pwait(pz_r.at[1])
    psend(slot(0, 1), pl.ds(2 * c + 1, 1), snd.at[S_PZH], pz_r.at[3], at_z(-1))
    ysend(1)
    ysend(2)
    pshare(slot(0, -1))
    pshare(slot(0, 1))
    pwait(pz_r.at[2], 1)
    pwait(pz_r.at[3], 1)
    ysend(3)
    zrun(2)
    pshare(slot(0, 2))
    for k in range(4, NY):
        ysend(k)
        zrun(PLAN_Y)
    drain(rall.at[0], one_r.at[R_RZ])
    for d in (1, -1, 2):
        rcopy(rall.at[other], rall.at[other], snd.at[S_RX2], one_r.at[R_RX2], at_x(d)).start()
    l_r.wait()
    rowsb[...] = rows[...].astype(BF16)
    for cp in l_a + l_o:
        cp.wait()

    def project(acc, dys):
        left, right = acc
        for dy in dys:
            for dz in (0, 1, 2, 3):
                i = slot(dy, dz)
                start = pl.multiple_of(448 * i - 64 * (i % 2), 128)
                w = ptall[i].reshape(64, PW)
                left = left + nt_dot(act[:, pl.ds(start, WIN)], w[:, :WIN])
                right = right + nt_dot(w[:, WIN:], og[:, pl.ds(pl.multiple_of(128 * i, 128), 128)])
        return left, right

    drain(ptall.at[pl.ds(0, 19), pl.ds(0, 2)], one_r.at[R_PSH])
    zrun(1)
    acc = project((jnp.zeros((64, 64), F32), jnp.zeros((64, 64), F32)), (0, -1, 1, -2, 2))
    yrecv_to(0, NY)
    yrecv_to(1, NY)
    zrun(1)
    drain(rall.at[pl.ds(0, 3)], one_r.at[R_RX])
    drain(ptall.at[pl.ds(0, 12), pl.ds(0, 2)], one_r.at[R_PSH2])
    left, right = project(acc, (-3, 3, 4))
    left = left.astype(BF16)
    right = right.astype(BF16)
    r0 = lax.broadcasted_iota(jnp.int32, (64, 64), 0)
    r1 = lax.broadcasted_iota(jnp.int32, (64, 64), 1)
    pick = (r1 == 2 * (r0 % 32) + r0 // 32).astype(F32).astype(BF16)
    right = jnp.dot(pick, right, preferred_element_type=F32)
    for d in range(2):
        live = valid_ref[pl.ds(d, 1), :].astype(F32)
        rest = jnp.zeros((1, 32), F32)
        masked = (right * jnp.concatenate([live, rest] if d == 0 else [rest, live], axis=1)).astype(BF16)
        outer = jnp.dot(masked, left, preferred_element_type=F32)
        part[:, d, :] = jnp.concatenate([outer[:32], outer[32:]], axis=1)

    l_pr.wait()
    drain(rall.at[pl.ds(0, 3)], one_r.at[R_RX2])

    @pl.loop(0, 8)
    def _(k):
        ref = rall.at[2 * k + c]
        rcopy(ref, ref, snd.at[S_RSH], one_r.at[R_RSH], partner).start()

    @pl.loop(1, NT)
    def _(k):
        to = (t + k) % NT
        rcopy(part.at[to], rsbuf.at[t], snd.at[S_RS], one_r.at[R_RS], (to, s)).start()

    rsbuf[t] = part[t]
    zrun(PLAN_RS)
    drain(rall.at[pl.ds(0, 8)], one_r.at[R_RSH])
    prows = rall[...].astype(F32).reshape(128, 4096).astype(BF16)
    own_q = jnp.concatenate(
        [jnp.concatenate([qall[s, k, j] for j in range(NSPLIT)], axis=1) for k in range(4)], axis=0
    )
    qp = nt_dot(own_q, prows).astype(BF16)
    drain(rsbuf.at[pl.ds(0, NT - 1)], one_r.at[R_RS])
    total = jnp.sum(rsbuf[...], axis=0) * (1.0 / 32.0)
    gown[...] = total.astype(BF16).astype(F32)
    gt[t] = gown[...]
    gs[s] = gown[...]

    @pl.loop(1, NS)
    def _(k):
        rcopy(gown, gs.at[s], snd.at[S_GS], one_r.at[R_GS], (t, (s + k) % NS)).start()

    @pl.loop(1, NT)
    def _(k):
        rcopy(gown, gt.at[t], snd.at[S_GT], one_r.at[R_GT], ((t + k) % NT, s)).start()

    zrun(PLAN_AG)
    drain(gs.at[pl.ds(0, NS - 1)], one_r.at[R_GS])
    docs = jnp.concatenate([gs[:, 0, :], gs[:, 1, :]], axis=0)
    acc = jnp.zeros((16, 128), F32)
    d0 = lax.broadcasted_iota(jnp.int32, (16, 32), 0)
    d1 = lax.broadcasted_iota(jnp.int32, (16, 32), 1)
    none = jnp.zeros((64, 128), BF16)
    for h in range(2):
        put = (d0 + 16 * h == 2 * (d1 % 16) + d1 // 16).astype(F32).astype(BF16)
        block = jnp.dot(put, docs.astype(BF16), preferred_element_type=F32).astype(BF16)
        acc = acc + nt_dot(block, jnp.concatenate([qp, none] if h == 0 else [none, qp], axis=0))
    arsrc[...] = acc
    ary[y] = acc

    @pl.loop(1, 8)
    def _(k):
        rcopy(arsrc, ary.at[y], snd.at[S_ARY], one_r.at[R_ARY], at_y(k)).start()

    zrun(PLAN_AR)
    drain(gt.at[pl.ds(0, NT - 1)], one_r.at[R_GT])
    pdoc_ref[...] = nt_dot(jnp.concatenate([gt[i] for i in range(NT)], axis=1).astype(BF16), prows)

    drain(ary.at[pl.ds(0, 7)], one_r.at[R_ARY])
    acc = jnp.sum(ary[...], axis=0)
    arsrc2[...] = acc
    arz[zl] = acc

    @pl.loop(1, 4)
    def _(k):
        rcopy(arsrc2, arz.at[zl], snd.at[S_ARZ], one_r.at[R_ARZ], (((zl + k) % 4) * 8 + y, s)).start()

    drain(qall.at[pl.ds(0, 4)], one_r.at[R_QSA])
    score(zh)
    zrun(nsteps)
    for n in range(4 * NSPLIT):
        ref = qall.at[(1 - zh) * 8 + ((x + 2) % 4) * 2 + c, n // NSPLIT, n % NSPLIT]
        drain(ref, xo_r.at[n])
        qshare(ref, R_QSB)
    drain(qall.at[pl.ds(0, 4)], one_r.at[R_QSB])
    score(1 - zh)

    drain(arz.at[pl.ds(0, 3)], one_r.at[R_ARZ])
    acc = jnp.sum(arz[...], axis=0)
    dsc_ref[...] = jnp.concatenate([acc[:, :64], acc[:, 64:]], axis=0)

    sent(ptall.at[pl.ds(0, 2), pl.ds(0, 2)], snd.at[S_PZ])
    sent(ptall.at[0, pl.ds(0, 2)], snd.at[S_PZH])
    sent(ptall.at[pl.ds(0, 2 * NY), pl.ds(0, 2)], snd.at[S_PY])
    sent(ptall.at[pl.ds(0, NT - 1), pl.ds(0, 2)], snd.at[S_PSH])
    sent(qall.at[pl.ds(0, 4)], snd.at[S_X])
    sent(qall.at[pl.ds(0, 3)], snd.at[S_Z])
    sent(qall.at[pl.ds(0, 8)], snd.at[S_QSH])
    sent(rall.at[0], snd.at[S_RZ])
    sent(rall.at[pl.ds(0, 3)], snd.at[S_RX])
    sent(rall.at[pl.ds(0, 3)], snd.at[S_RX2])
    sent(rall.at[pl.ds(0, 8)], snd.at[S_RSH])
    sent(rsbuf.at[pl.ds(0, NT - 1)], snd.at[S_RS])
    sent(gt.at[pl.ds(0, NT - 1)], snd.at[S_GT])
    sent(gs.at[pl.ds(0, NS - 1)], snd.at[S_GS])
    sent(ary.at[pl.ds(0, 7)], snd.at[S_ARY])
    sent(arz.at[pl.ds(0, 3)], snd.at[S_ARZ])


def hand_over(a_ref, b_ref, c_ref, a_out, b_out, c_out):
    a_out[...] = a_ref[...]
    b_out[...] = b_ref[...]
    c_out[...] = c_ref[...]


def local(activations, out_grads, validity, proj_in, proj_out, precond, queries, store_rows, plan):
    hbm = pl.BlockSpec(memory_space=pl.ANY)
    vm = pl.BlockSpec(memory_space=pltpu.VMEM)
    sm = pl.BlockSpec(memory_space=pltpu.SMEM)
    dma = pltpu.SemaphoreType.DMA
    made = pl.pallas_call(
        kernel,
        out_shape=(
            jax.ShapeDtypeStruct((1024, 128), F32),
            jax.ShapeDtypeStruct((2, 128), F32),
            jax.ShapeDtypeStruct((32, 64), F32),
        ),
        in_specs=[sm, vm, vm, vm, hbm, hbm, hbm, hbm, hbm],
        out_specs=(vm, vm, vm),
        scratch_shapes=[
            pltpu.VMEM((NT, 4, 16, PW), BF16),
            pltpu.VMEM((64, 14336), BF16),
            pltpu.VMEM((64, 4096), BF16),
            pltpu.VMEM((128, 4096), F32),
            pltpu.VMEM((128, 4096), BF16),
            pltpu.VMEM((NS, 4, NSPLIT, 16, ZCOLS), BF16),
            pltpu.VMEM((NS, 8, 4096), BF16),
            pltpu.VMEM((NT, 2, 128), F32),
            pltpu.VMEM((NT, 2, 128), F32),
            pltpu.VMEM((2, 128), F32),
            pltpu.VMEM((NT, 2, 128), F32),
            pltpu.VMEM((NS, 2, 128), F32),
            pltpu.VMEM((8, 16, 128), F32),
            pltpu.VMEM((4, 16, 128), F32),
            pltpu.VMEM((16, 128), F32),
            pltpu.VMEM((16, 128), F32),
            dma((6,)),
            dma((4,)),
            dma((NY,)),
            dma((NY,)),
            dma((4, 4, NSPLIT)),
            dma((NZ,)),
            dma((NZ,)),
            dma((4 * NSPLIT,)),
            dma((13,)),
            dma((16,)),
        ],
        compiler_params=pltpu.CompilerParams(collective_id=0, has_side_effects=True),
        name="logra",
    )(
        plan.reshape(16),
        validity,
        proj_in.T,
        proj_out.T,
        activations,
        out_grads,
        precond,
        queries.reshape(4, 16, 4096),
        store_rows,
    )
    scores, precond_docs, doc_scores = pl.pallas_call(
        hand_over,
        out_shape=tuple(jax.ShapeDtypeStruct(m.shape, m.dtype) for m in made),
        in_specs=[vm] * 3,
        out_specs=(vm,) * 3,
        name="hand_over",
    )(*made)
    return scores, precond_docs, doc_scores.T


def solution(mesh):
    return jax.shard_map(
        local,
        mesh=mesh,
        in_specs=(
            P("store", "tok", None),
            P("store", "tok", None),
            P("store", "tok"),
            P("tok", None),
            P("tok", None),
            P(("tok", "store"), None),
            P("store", None),
            P(("tok", "store"), None),
            P(None, ("tok", "store")),
        ),
        out_specs=(P(None, ("tok", "store")), P("store", "tok"), P("store", None)),
        check_vma=False,
    )
```
